512 devices in a mesh: ep: 128 (over y, z, core), tp: 4 (over x).
Axes of the slice: x: 4, y: 8, z: 8, core: 2. Of those that a mesh axis runs over, the one named last changes fastest.
Arguments:
- queries: bfloat16 [8192, 2048], P('ep', 'tp'), may hold values from -1024 to 1024
- new_keys: bfloat16 [8192, 512], P('ep', 'tp'), may hold values from -6 to 6
- new_values: bfloat16 [8192, 512], P('ep', 'tp'), may hold values from -5 to 5
- key_cache: bfloat16 [128, 512, 512], P('ep', None, 'tp'), may hold values from -5 to 5
- value_cache: bfloat16 [128, 512, 512], P('ep', None, 'tp'), may hold values from -5 to 5
- cache_lengths: int32 [128], P('ep'), may hold values from 1 to 512, 32768 in all
- request_order: int32 [128], replicated, may hold values from 0 to 127, each once
- residual: bfloat16 [8192, 2048], P('ep', 'tp'), may hold values from -6 to 6
- out_weight: bfloat16 [2048, 2048], P('tp'), may hold values from -0.125 to 0.125
- norm_gain: float32 [2048], replicated, may hold values from 0.1 to 1.9
- route_experts: int32 [8192, 8], P('ep'), may hold values from 0 to 127, all different within a row; in each aligned block of 64 rows (0 to 63, 64 to 127, ...) at most 8 rows name the same one
- route_weights: float32 [8192, 8], P('ep'), may hold values from 0.1 to 1
- expert_gate: bfloat16 [128, 2048, 768], P('ep', None, 'tp'), may hold values from -0.125 to 0.125
- expert_up: bfloat16 [128, 2048, 768], P('ep', None, 'tp'), may hold values from -0.125 to 0.125
- expert_down: bfloat16 [128, 768, 2048], P('ep', None, 'tp'), may hold values from -0.21875 to 0.21875
Outputs:
- output: bfloat16 [8192, 2048], P('ep', 'tp')
The draws below stay inside these ranges and needn't reach their ends.
Inputs may be any that keep to these rules, and one draw needn't show every extreme that they name: `cache_lengths`: the longest cache holds exactly 512 rows in every draw. `request_order`: each request block appears once. `route_experts`: each row names 8 different experts; within each request's block of 64 rows no expert is named by more than 8 rows, a bound that some block reaches.
All inputs are finite; a program needn't handle non-finite values. No bound on the sum of `cache_lengths` on one device may be relied on, other than what follows from the above.
Results may differ from the reference program's by a relative error of at most 0.0057.
Values may be sent and summed in bfloat16 or wider, within the bound.
A program may use at most 64 MiB of HBM per device.

```python
import math
import jax
import jax.numpy as jnp
import numpy as np
from jax import lax

D = 2048
HEAD = 128
QHEADS = 16
KVHEADS = 4
FF = 768
TOK_DEV = 64
CACHE = 512
REQS = 128
TOKENS = 8192
EXPERTS = 128
TOP = 8
CAP = 8


def cached_keys_draw(key):
    folded = jax.random.fold_in(key, 7)
    dims_all = (REQS, CACHE, KVHEADS * HEAD)
    values = jnp.clip(jax.random.normal(folded, dims_all, jnp.float32), -5.0, 5.0)
    return values


def draw_key_cache(key, part):
    return cached_keys_draw(key).astype(jnp.bfloat16)


def draw_new_keys(key, part):
    drawn = jnp.clip(jax.random.normal(jax.random.fold_in(key, 11), (TOKENS, KVHEADS * HEAD), jnp.float32), -5.0, 5.0)
    return drawn.astype(jnp.bfloat16)


def draw_queries(key, part):
    drawn = jnp.clip(jax.random.normal(jax.random.fold_in(key, 13), (REQS, TOK_DEV, QHEADS, HEAD), jnp.float32), -5.0, 5.0)
    return drawn.reshape(TOKENS, QHEADS * HEAD).astype(jnp.bfloat16)


def level_of(rng, dims, shards, least, largest):
    def one(dim, parts):
        steps = jax.random.uniform(jax.random.fold_in(jax.random.fold_in(rng, 6), dim), (parts,), jnp.float32, least / len(shards), largest / len(shards))
        return jnp.repeat(jnp.exp(steps), dims[dim] // parts).reshape((-1,) + (1,) * (len(dims) - dim - 1))

    gain = one(*shards[0])
    for cut in shards[1:]:
        gain = gain * one(*cut)
    return gain


def profile(amount, total, limit, slope):
    weights = [(1 << 20) // math.isqrt(grade ** slope) + 1 for grade in range(2, amount + 1)]
    surplus, counts = total - limit - (amount - 1), [1] * (amount - 1)
    while surplus > 0:
        movable = [i for i in range(amount - 1) if counts[i] < limit]
        whole, budget = sum([weights[i] for i in movable]), surplus
        for i in movable:
            addition = min(limit - counts[i], max(1, budget * weights[i] // whole), surplus)
            counts[i] = counts[i] + addition
            surplus = surplus - addition
    return np.array([limit] + counts)


def ragged(stream_key, count, total, limit, skew):
    if count == 2:
        one = jax.random.randint(stream_key, (), max(1, total - limit), min(limit, total - 1) + 1)
        return jnp.stack([one, total - one])
    tallies = jnp.asarray(profile(count, total, limit, skew), jnp.int32)
    couples = (count - 1) // 2
    giver, sink = tallies[1:1 + 2 * couples:2], tallies[2:2 + 2 * couples:2]
    slack = jnp.minimum(giver - 1, limit - sink)
    passed = jax.random.randint(jax.random.fold_in(stream_key, 1), (couples,), 0, 1 << 20) % (slack + 1)
    tallies = tallies.at[1:1 + 2 * couples:2].set(giver - passed).at[2:2 + 2 * couples:2].set(sink + passed)
    return tallies[jax.random.permutation(jax.random.fold_in(stream_key, 2), count)]


def assign_block(rng, own, number, rows, count, top, reach, lean):
    order = jax.random.permutation(rng, count)
    heavy_load, usual = load_shares(count, rows * top, reach, lean, True), load_shares(count, rows * top, reach, lean, False)
    places = jnp.arange(count)

    def named(sizes, turn):
        used = int((sizes > 0).sum())
        fixed = max(1, used // 4)
        shifted = fixed + (places - fixed + turn * (used - fixed)) % max(1, count - fixed)
        return jnp.zeros((count,), jnp.int32).at[order[jnp.where(places < fixed, places, shifted)]].set(jnp.asarray(sizes, jnp.int32))

    sizes = jnp.where(number % 4 == 0, named(heavy_load, number // 4), named(usual, number - number // 4 - 1))
    mixed = jax.random.permutation(jax.random.fold_in(own, 3), count)
    giver, taker = mixed[0:count // 2 * 2:2], mixed[1:count // 2 * 2:2]
    room = jnp.minimum(sizes[giver] - 1, reach - sizes[taker]) // 2
    room = jnp.where((giver == order[0]) | (taker == order[0]) | (sizes[taker] == 0), 0, jnp.maximum(room, 0))
    shifted = jax.random.randint(jax.random.fold_in(own, 4), (count // 2,), 0, 1 << 20) % (room + 1)
    sizes = sizes.at[giver].add(-shifted).at[taker].add(shifted)
    members = jnp.searchsorted(jnp.cumsum(sizes), jnp.arange(rows * top), side="right").astype(jnp.int32)
    listing = members.reshape(top, rows).T
    listing = listing[jax.random.permutation(jax.random.fold_in(own, 1), rows)]
    turn = jax.random.randint(jax.random.fold_in(own, 2), (rows, 1), 0, top)
    return jnp.take_along_axis(listing, (jnp.arange(top)[None, :] + turn) % top, axis=1)


def load_shares(count, total, bound, slope, full):
    weights = [(1 << 20) // math.isqrt(grade ** slope) + 1 for grade in range(1, count + 1)]
    largest = bound if full else min(bound, max(-(-total // count), total * weights[0] // sum(weights)))
    least = 1 if total - largest >= count - 1 else 0
    holding, spare = [largest] + [least] * (count - 1), total - largest - least * (count - 1)
    while spare > 0:
        free = [i for i in range(1, count) if holding[i] < largest] or [i for i in range(1, count) if holding[i] < bound]
        mass, left = sum([weights[i] for i in free]), spare
        for i in free:
            extra = min(bound - holding[i], max(1, left * weights[i] // mass), spare)
            holding[i] = holding[i] + extra
            spare = spare - extra
    return np.array(holding)


def bell_draw(rng, extent, width, reach, shards=(), held_as=jnp.bfloat16):
    level = level_of(rng, extent, shards, -0.22, 0.18) if shards else 1.0
    values = jax.random.normal(rng, extent, jnp.float32) * width * level
    return jnp.minimum(jnp.maximum(values, -reach), reach).astype(held_as)


def setup_inputs(seed: int = 0) -> dict:
    splits = jax.random.split(jax.random.key(seed), 16)
    queries = draw_queries(jax.random.fold_in(splits[15], 71), 0)
    new_keys = draw_new_keys(jax.random.fold_in(splits[15], 71), 0)
    new_values = bell_draw(splits[2], (TOKENS, KVHEADS * HEAD), 1.0, 5.0, ((0, 128), (1, 4)))
    key_cache = draw_key_cache(jax.random.fold_in(splits[15], 71), 0)
    value_cache = bell_draw(splits[4], (REQS, CACHE, KVHEADS * HEAD), 1.0, 5.0, ((0, 128), (2, 4)))
    cache_lengths = ragged(splits[5], REQS, REQS * CACHE // 2, CACHE, 2).astype(jnp.int32)
    request_order = jax.random.permutation(splits[6], REQS).astype(jnp.int32)
    residual = bell_draw(splits[7], (TOKENS, D), 1.0, 6.0, ((0, 128), (1, 4)))
    out_weight = bell_draw(splits[8], (QHEADS * HEAD, D), (QHEADS * HEAD) ** -0.5, 0.125, ((0, 4),))
    norm_gain = jnp.clip(1.0 + 0.18 * jax.random.normal(splits[9], (D,), jnp.float32), 0.1, 1.9)
    route_experts_keys = jax.random.split(jax.random.fold_in(splits[10], 1), TOKENS // TOK_DEV)
    route_experts_turns = jax.random.permutation(jax.random.fold_in(splits[10], 3), TOKENS // TOK_DEV)
    route_experts = jax.vmap(lambda own, number: assign_block(jax.random.fold_in(splits[10], 2), own, number, TOK_DEV, EXPERTS, TOP, CAP, 2))(route_experts_keys, route_experts_turns).reshape((TOKENS, TOP))
    route_weights = jnp.clip(jnp.exp(math.log(1.0) - 2.3025851 * jax.random.uniform(splits[11], (TOKENS, TOP), jnp.float32) ** level_of(splits[11], (TOKENS, TOP), ((0, 128),), -0.2, 0.2)), 0.1, 1.0)
    expert_gate = bell_draw(splits[12], (EXPERTS, D, FF), D ** -0.5, 0.125, ((0, 128), (2, 4)))
    expert_up = bell_draw(splits[13], (EXPERTS, D, FF), D ** -0.5, 0.125, ((0, 128), (2, 4)))
    expert_down = bell_draw(splits[14], (EXPERTS, FF, D), FF ** -0.5, 0.21875, ((0, 128), (2, 4)))
    return {"queries": queries, "new_keys": new_keys, "new_values": new_values, "key_cache": key_cache, "value_cache": value_cache, "cache_lengths": cache_lengths, "request_order": request_order, "residual": residual, "out_weight": out_weight, "norm_gain": norm_gain, "route_experts": route_experts, "route_weights": route_weights, "expert_gate": expert_gate, "expert_up": expert_up, "expert_down": expert_down}


def attend_request(operands):
    query_rows, key_rows, value_rows, cached_keys, cached_values, length = operands
    group_size = QHEADS // KVHEADS
    query_view = query_rows.astype(jnp.float32).reshape(TOK_DEV, KVHEADS, group_size, HEAD)
    all_keys = jnp.concatenate([cached_keys, key_rows], axis=0).astype(jnp.float32).reshape(CACHE + TOK_DEV, KVHEADS, HEAD)
    all_values = jnp.concatenate([cached_values, value_rows], axis=0).astype(jnp.float32).reshape(CACHE + TOK_DEV, KVHEADS, HEAD)
    scores = jnp.einsum('tghd,kgd->tghk', query_view, all_keys) / math.sqrt(HEAD)
    position = jnp.arange(CACHE + TOK_DEV, dtype=jnp.int32)
    current = jnp.arange(TOK_DEV, dtype=jnp.int32)
    visible = jnp.where(position[None, :] < CACHE, position[None, :] < length, position[None, :] - CACHE <= current[:, None])
    visible = visible[:, None, None, :]
    highest = lax.optimization_barrier(jnp.max(jnp.where(visible, scores, -1e+30), axis=-1, keepdims=True))
    raised = jnp.exp(jnp.where(visible, scores - highest, -1e+30))
    totals = lax.optimization_barrier(jnp.sum(raised, axis=-1, keepdims=True))
    rounded = lax.optimization_barrier(raised.astype(jnp.bfloat16)).astype(jnp.float32)
    context = jnp.einsum('tghk,kgd->tghd', rounded, all_values) / totals
    return context.astype(jnp.bfloat16).reshape(TOK_DEV, QHEADS * HEAD)

def reference(queries, new_keys, new_values, key_cache, value_cache, cache_lengths, request_order, residual, out_weight, norm_gain, route_experts, route_weights, expert_gate, expert_up, expert_down):
    contexts = lax.map(attend_request, (queries.reshape(REQS, TOK_DEV, -1), new_keys.reshape(REQS, TOK_DEV, -1), new_values.reshape(REQS, TOK_DEV, -1), key_cache, value_cache, cache_lengths))
    context = contexts.reshape(TOKENS, QHEADS * HEAD)
    attended = jnp.dot(context, out_weight, preferred_element_type=jnp.float32)
    hidden_state = (residual.astype(jnp.float32) + attended).astype(jnp.bfloat16)
    widened = hidden_state.astype(jnp.float32)
    mean_square = lax.optimization_barrier(jnp.mean(widened * widened, axis=-1, keepdims=True))
    normed = (widened * lax.rsqrt(mean_square + 1e-06) * norm_gain).astype(jnp.bfloat16)
    mixing = (route_weights / lax.optimization_barrier(jnp.sum(route_weights, axis=-1, keepdims=True))).astype(jnp.bfloat16)
    flat_routes = route_experts.reshape(REQS, TOK_DEV * TOP)
    onehot = (flat_routes[:, :, None] == jnp.arange(EXPERTS, dtype=jnp.int32)[None, None, :]).astype(jnp.int32)
    ranking = lax.optimization_barrier(jnp.sum(jnp.cumsum(onehot, axis=1) * onehot, axis=2)) - 1
    request_ids = jnp.broadcast_to(jnp.arange(REQS, dtype=jnp.int32)[:, None], flat_routes.shape)
    token_ids = request_ids * TOK_DEV + jnp.arange(TOK_DEV * TOP, dtype=jnp.int32)[None, :] // TOP
    table_tokens = jnp.full((EXPERTS, REQS, CAP), -1, jnp.int32).at[flat_routes, request_ids, ranking].set(token_ids)
    table_mix = jnp.zeros((EXPERTS, REQS, CAP), jnp.bfloat16).at[flat_routes, request_ids, ranking].set(mixing.reshape(REQS, TOK_DEV * TOP))

    def expert_step(running, operands):
        weights_gate, weights_up, weights_down, token_list, mix_list = operands
        present = token_list >= 0
        safe_ids = jnp.where(present, token_list, 0)
        inputs = normed[safe_ids]
        gate_value = jnp.dot(inputs, weights_gate, preferred_element_type=jnp.float32)
        up_value = jnp.dot(inputs, weights_up, preferred_element_type=jnp.float32)
        activation = (jax.nn.silu(gate_value) * up_value).astype(jnp.bfloat16)
        expert_out = jnp.dot(activation, weights_down, preferred_element_type=jnp.float32)
        contribution = (mix_list.astype(jnp.float32)[:, None] * (widened[safe_ids] + expert_out)).astype(jnp.bfloat16)
        contribution = lax.optimization_barrier(contribution).astype(jnp.float32)
        contribution = jnp.where(present[:, None], contribution, 0.0)
        return (running.at[safe_ids].add(contribution), None)
    initial = jnp.zeros((TOKENS, D), jnp.float32)
    summed, _ = lax.scan(expert_step, initial, (expert_gate, expert_up, expert_down, table_tokens.reshape(EXPERTS, REQS * CAP), table_mix.reshape(EXPERTS, REQS * CAP)))
    placed = jnp.zeros((REQS, TOK_DEV, D), jnp.float32).at[request_order].set(summed.reshape(REQS, TOK_DEV, D))
    return placed.reshape(TOKENS, D).astype(jnp.bfloat16)
```

```python
import functools
import math

import jax
import jax.numpy as jnp
from jax import lax
from jax.experimental import pallas as pl
from jax.experimental.pallas import tpu as pltpu
from jax.sharding import PartitionSpec as P

HEAD = 128
QHEADS = 16
KVHEADS = 4
CAP = 8
STRIDE = 37
LAG = 4
MESH = pl.DeviceIdType.MESH


def attention_block(queries, new_keys, new_values, key_cache, value_cache, cache_lengths, kv_local):
    tokens_here = queries.shape[0]
    cached = key_cache.shape[1]
    group_size = QHEADS // KVHEADS
    query_view = queries.reshape(tokens_here, kv_local, group_size, HEAD)
    all_keys = jnp.concatenate([key_cache[0], new_keys], axis=0).reshape(
        cached + tokens_here, kv_local, HEAD
    )
    all_values = jnp.concatenate([value_cache[0], new_values], axis=0).reshape(
        cached + tokens_here, kv_local, HEAD
    )
    scores = jnp.einsum(
        "tghd,kgd->tghk", query_view, all_keys, preferred_element_type=jnp.float32
    ) / math.sqrt(HEAD)
    position = jnp.arange(cached + tokens_here, dtype=jnp.int32)
    current = jnp.arange(tokens_here, dtype=jnp.int32)
    visible = jnp.where(
        position[None, :] < cached,
        position[None, :] < cache_lengths[0],
        position[None, :] - cached <= current[:, None],
    )
    visible = visible[:, None, None, :]
    highest = jnp.max(jnp.where(visible, scores, -1e30), axis=-1, keepdims=True)
    raised = jnp.exp(jnp.where(visible, scores - highest, -1e30))
    totals = jnp.sum(raised, axis=-1, keepdims=True)
    weights = raised.astype(jnp.bfloat16)
    context = (
        jnp.einsum("tghk,kgd->tghd", weights, all_values, preferred_element_type=jnp.float32)
        / totals
    )
    return context.astype(jnp.bfloat16).reshape(tokens_here, -1)


def exchange_kernel(tps, x_ref, out_ref, send_sem, recv_sem, own_sem):
    tp = lax.axis_index("tp")
    width = out_ref.shape[2]
    barrier = pltpu.get_barrier_semaphore()
    for o in range(1, tps):
        pl.semaphore_signal(
            barrier, inc=1, device_id={"tp": lax.rem(tp + o, tps)}, device_id_type=MESH
        )
    own = pltpu.make_async_copy(
        x_ref.at[:, pl.ds(pl.multiple_of(tp * width, width), width)], out_ref.at[0], own_sem
    )
    own.start()
    pl.semaphore_wait(barrier, tps - 1)
    copies = []
    for o in range(1, tps):
        peer = lax.rem(tp + o, tps)
        copy = pltpu.make_async_remote_copy(
            src_ref=x_ref.at[:, pl.ds(pl.multiple_of(peer * width, width), width)],
            dst_ref=out_ref.at[o],
            send_sem=send_sem.at[o - 1],
            recv_sem=recv_sem.at[o - 1],
            device_id={"tp": peer},
            device_id_type=MESH,
        )
        copy.start()
        copies.append(copy)
    own.wait()
    for copy in copies:
        copy.wait()


def exchange(terms, tps):
    rows, total = terms.shape
    return pl.pallas_call(
        functools.partial(exchange_kernel, tps),
        out_shape=jax.ShapeDtypeStruct((tps, rows, total // tps), terms.dtype),
        in_specs=[pl.BlockSpec(memory_space=pltpu.VMEM)],
        out_specs=pl.BlockSpec(memory_space=pltpu.VMEM),
        scratch_shapes=[
            pltpu.SemaphoreType.DMA((tps - 1,)),
            pltpu.SemaphoreType.DMA((tps - 1,)),
            pltpu.SemaphoreType.DMA,
        ],
        compiler_params=pltpu.CompilerParams(collective_id=0, has_side_effects=True),
        name="tp_exchange",
    )(terms)


def slot_matrices(experts, mix, count):
    tokens, top = experts.shape
    lanes = lax.broadcasted_iota(jnp.int32, (tokens, count), 1)
    named = jnp.zeros((tokens, count), jnp.float32)
    mixed = jnp.zeros((tokens, count), jnp.float32)
    for k in range(top):
        hit = experts[:, k : k + 1] == lanes
        named = jnp.where(hit, 1.0, named)
        mixed = jnp.where(hit, mix[:, k : k + 1], mixed)
    row = lax.broadcasted_iota(jnp.int32, (tokens, tokens), 0)
    col = lax.broadcasted_iota(jnp.int32, (tokens, tokens), 1)
    earlier = jnp.where(col < row, 1.0, 0.0).astype(jnp.bfloat16)
    rank = jnp.dot(earlier, named.astype(jnp.bfloat16), preferred_element_type=jnp.float32)
    marked = jnp.where(named > 0.0, rank, 255.0).astype(jnp.bfloat16)
    source = lax.broadcasted_iota(jnp.int32, (count, count * CAP), 0)
    target = lax.broadcasted_iota(jnp.int32, (count, count * CAP), 1)
    spread = jnp.where(target // CAP == source, 1.0, 0.0).astype(jnp.bfloat16)
    rank_wide = jnp.dot(marked, spread, preferred_element_type=jnp.float32)
    mix_wide = jnp.dot(mixed.astype(jnp.bfloat16), spread, preferred_element_type=jnp.float32)
    place = lax.rem(
        lax.broadcasted_iota(jnp.int32, (tokens, count * CAP), 1), CAP
    ).astype(jnp.float32)
    chosen = rank_wide == place
    selector = jnp.where(chosen, 1.0, 0.0).astype(jnp.bfloat16)
    weighted = jnp.where(chosen, mix_wide, 0.0).astype(jnp.bfloat16)
    return selector, weighted


def prepare_kernel(count, terms_ref, residual_ref, experts_ref, out_ref):
    total = residual_ref[...].astype(jnp.float32)
    for o in range(terms_ref.shape[0]):
        total = total + terms_ref[o].astype(jnp.float32)
    hidden = total.astype(jnp.bfloat16)
    experts = experts_ref[...]
    selector, _ = slot_matrices(experts, experts.astype(jnp.float32), count)
    rows = lax.dot_general(
        selector, hidden, (((0,), (0,)), ((), ())), preferred_element_type=jnp.float32
    )
    out_ref[...] = rows.reshape(out_ref.shape).astype(jnp.bfloat16)


def prepare(terms, residual, experts, count):
    return pl.pallas_call(
        functools.partial(prepare_kernel, count),
        out_shape=jax.ShapeDtypeStruct((count, CAP, residual.shape[1]), jnp.bfloat16),
        name="prepare",
    )(terms, residual, experts)


def dispatch_kernel(
    eps,
    tps,
    send_ref,
    meta_ref,
    full_ref,
    metas_ref,
    own_sem,
    send_sem,
    meta_send,
    meta_recv,
    recv_sem,
    right_send,
    left_send,
    left_recv,
    right_recv,
    relay_send,
    relay_recv,
):
    ep = lax.axis_index("ep")
    tp = lax.axis_index("tp")
    right = lax.rem(tp + 1, tps)
    left = lax.rem(tp + tps - 1, tps)
    barrier = pltpu.get_barrier_semaphore()

    def greet(k, carry):
        pl.semaphore_signal(
            barrier, inc=1, device_id={"ep": lax.rem(ep + k, eps)}, device_id_type=MESH
        )
        return carry

    for side in (right, left):
        pl.semaphore_signal(barrier, inc=1, device_id={"tp": side}, device_id_type=MESH)
    lax.fori_loop(1, eps, greet, 0)
    own = pltpu.make_async_copy(send_ref.at[ep], full_ref.at[tp, ep], recv_sem.at[0])
    own.start()
    own_meta = pltpu.make_async_copy(meta_ref, metas_ref.at[ep], own_sem)
    own_meta.start()
    pl.semaphore_wait(barrier, eps + 1)

    def offset(k):
        return lax.rem(k * STRIDE, eps)

    def post(k, carry):
        off = offset(k)
        dst = lax.rem(ep + off, eps)
        pltpu.make_async_remote_copy(
            src_ref=send_ref.at[dst],
            dst_ref=full_ref.at[tp, ep],
            send_sem=send_sem,
            recv_sem=recv_sem.at[off],
            device_id={"ep": dst},
            device_id_type=MESH,
        ).start()
        return carry

    def post_meta(k, carry):
        pltpu.make_async_remote_copy(
            src_ref=meta_ref,
            dst_ref=metas_ref.at[ep],
            send_sem=meta_send,
            recv_sem=meta_recv,
            device_id={"ep": lax.rem(ep + offset(k), eps)},
            device_id_type=MESH,
        ).start()
        return carry

    lax.fori_loop(1, eps, post, 0)
    lax.fori_loop(1, eps, post_meta, 0)

    def source(k):
        return lax.rem(ep + eps - offset(k), eps)

    def spread(k):
        src = source(k)
        block = full_ref.at[tp, src]
        pltpu.make_async_copy(block, block, recv_sem.at[offset(k)]).wait()
        for side, ssem, rsem in ((right, right_send, left_recv), (left, left_send, right_recv)):
            pltpu.make_async_remote_copy(
                src_ref=block,
                dst_ref=block,
                send_sem=ssem,
                recv_sem=rsem.at[k],
                device_id={"tp": side},
                device_id_type=MESH,
            ).start()

    def relay(k, way):
        src = source(k)
        from_left = full_ref.at[left, src]
        from_right = full_ref.at[right, src]
        pltpu.make_async_copy(from_left, from_left, left_recv.at[k]).wait()
        pltpu.make_async_copy(from_right, from_right, right_recv.at[k]).wait()
        block, side = ((from_left, right), (from_right, left))[way]
        pltpu.make_async_remote_copy(
            src_ref=block,
            dst_ref=block,
            send_sem=relay_send.at[way],
            recv_sem=relay_recv.at[way],
            device_id={"tp": side},
            device_id_type=MESH,
        ).start()

    for k in range(LAG):
        spread(k)

    def step(i, carry):
        for way in range(2):
            spread(2 * i + way + LAG)
            relay(2 * i + way, way)
        return carry

    lax.fori_loop(0, (eps - LAG) // 2, step, 0)
    for k in range(eps - LAG, eps):
        relay(k, k % 2)

    def drain(ref, sem):
        pltpu.make_async_copy(ref, ref, sem).wait()

    own_meta.wait()
    most = send_ref.at[pl.ds(0, eps - 1)]
    drain(most, send_sem)
    drain(metas_ref.at[pl.ds(0, eps - 1)], meta_send)
    drain(metas_ref.at[pl.ds(0, eps - 1)], meta_recv)
    drain(send_ref, right_send)
    drain(send_ref, left_send)
    half = send_ref.at[pl.ds(0, eps // 2)]
    for way in range(2):
        drain(half, relay_send.at[way])
        drain(half, relay_recv.at[way])


def dispatch(send, meta, eps, tps):
    dma = pltpu.SemaphoreType.DMA
    return pl.pallas_call(
        functools.partial(dispatch_kernel, eps, tps),
        out_shape=(
            jax.ShapeDtypeStruct((tps,) + send.shape, send.dtype),
            jax.ShapeDtypeStruct((eps,) + meta.shape, meta.dtype),
        ),
        in_specs=[pl.BlockSpec(memory_space=pl.ANY)] * 2,
        out_specs=(pl.BlockSpec(memory_space=pl.ANY),) * 2,
        scratch_shapes=[
            dma, dma, dma, dma, dma((eps,)), dma, dma, dma((eps,)), dma((eps,)), dma((2,)), dma((2,))
        ],
        compiler_params=pltpu.CompilerParams(collective_id=1, has_side_effects=True),
        name="dispatch",
    )(send, meta)


def expert_in_kernel(rows_ref, gain_ref, gate_ref, up_ref, out_ref):
    parts, sources, cap, width = rows_ref.shape
    rows = sources * cap
    total = parts * width
    wide = [rows_ref[p].astype(jnp.float32).reshape(rows, width) for p in range(parts)]
    squares = sum(jnp.sum(part * part, axis=1, keepdims=True) for part in wide)
    factor = lax.rsqrt(squares / total + 1e-06)
    normed = jnp.concatenate(
        [
            (part * factor * gain_ref[:, p * width : (p + 1) * width]).astype(jnp.bfloat16)
            for p, part in enumerate(wide)
        ],
        axis=1,
    )
    dims = (((0,), (1,)), ((), ()))
    gate = lax.dot_general(gate_ref[...], normed, dims, preferred_element_type=jnp.float32)
    up = lax.dot_general(up_ref[...], normed, dims, preferred_element_type=jnp.float32)
    out_ref[...] = (gate / (1.0 + jnp.exp(-gate)) * up).astype(jnp.bfloat16)


def expert_in(full, gain, gate, up):
    parts, sources, cap, width = full.shape
    tiles = 4 if sources >= 64 else 1
    part_rows = sources // tiles
    ff = gate.shape[1]
    return pl.pallas_call(
        expert_in_kernel,
        grid=(tiles,),
        out_shape=jax.ShapeDtypeStruct((ff, sources * cap), jnp.bfloat16),
        in_specs=[
            pl.BlockSpec((parts, part_rows, cap, width), lambda i: (0, i, 0, 0)),
            pl.BlockSpec((1, gain.shape[1]), lambda i: (0, 0)),
            pl.BlockSpec(gate.shape, lambda i: (0, 0)),
            pl.BlockSpec(up.shape, lambda i: (0, 0)),
        ],
        out_specs=pl.BlockSpec((ff, part_rows * cap), lambda i: (0, i)),
        name="expert_in",
    )(full, gain, gate, up)


def gather_kernel(tps, chunks, x_ref, out_ref, own_sem, send_sem, recv_sem, relay_send, relay_recv):
    tp = lax.axis_index("tp")
    right = lax.rem(tp + 1, tps)
    left = lax.rem(tp + tps - 1, tps)
    sides = (right, left)
    barrier = pltpu.get_barrier_semaphore()
    for side in sides:
        pl.semaphore_signal(barrier, inc=1, device_id={"tp": side}, device_id_type=MESH)
    own = pltpu.make_async_copy(x_ref, out_ref.at[tp], own_sem)
    own.start()
    pl.semaphore_wait(barrier, 2)
    size = x_ref.shape[0] // chunks
    copies = []
    for c in range(chunks):
        part = pl.ds(c * size, size)
        pair = []
        for way in range(2):
            copy = pltpu.make_async_remote_copy(
                src_ref=x_ref.at[part],
                dst_ref=out_ref.at[tp, part],
                send_sem=send_sem.at[way, c],
                recv_sem=recv_sem.at[way, c],
                device_id={"tp": sides[way]},
                device_id_type=MESH,
            )
            copy.start()
            pair.append(copy)
        copies.append(pair)
    relays = []
    for c in range(chunks):
        part = pl.ds(c * size, size)
        way = c % 2
        for pair in copies[c]:
            pair.wait_recv()
        block = out_ref.at[(left, right)[way], part]
        copy = pltpu.make_async_remote_copy(
            src_ref=block,
            dst_ref=block,
            send_sem=relay_send.at[c],
            recv_sem=relay_recv.at[c],
            device_id={"tp": sides[way]},
            device_id_type=MESH,
        )
        copy.start()
        relays.append(copy)
    own.wait()
    for pair in copies:
        for copy in pair:
            copy.wait_send()
    for copy in relays:
        copy.wait()


def gather(x, tps):
    chunks = 4 if x.shape[0] % 64 == 0 else 2
    dma = pltpu.SemaphoreType.DMA
    return pl.pallas_call(
        functools.partial(gather_kernel, tps, chunks),
        out_shape=jax.ShapeDtypeStruct((tps,) + x.shape, x.dtype),
        in_specs=[pl.BlockSpec(memory_space=pltpu.VMEM)],
        out_specs=pl.BlockSpec(memory_space=pltpu.VMEM),
        scratch_shapes=[dma, dma((2, chunks)), dma((2, chunks)), dma((chunks,)), dma((chunks,))],
        compiler_params=pltpu.CompilerParams(collective_id=2, has_side_effects=True),
        name="tp_gather",
    )(x)


def expert_out_kernel(order_ref, act_ref, down_ref, own_ref, out_ref):
    sources, cap, width = own_ref.shape
    base = pl.program_id(0) * sources
    value = lax.dot_general(
        act_ref[...], down_ref[...], (((0,), (0,)), ((), ())), preferred_element_type=jnp.float32
    )
    value = value.reshape(sources, cap, width) + own_ref[...].astype(jnp.float32)
    value = value.astype(jnp.bfloat16)
    for j in range(sources):
        out_ref[order_ref[base + j]] = value[j]


def expert_out(order, act, down, full, tp):
    parts, sources, cap, width = full.shape
    tiles = 4 if sources >= 64 else 1
    part_rows = sources // tiles
    return pl.pallas_call(
        lambda order_ref, tp_ref, act_ref, down_ref, own_ref, out_ref: expert_out_kernel(
            order_ref, act_ref, down_ref, own_ref, out_ref
        ),
        grid_spec=pltpu.PrefetchScalarGridSpec(
            num_scalar_prefetch=2,
            grid=(tiles,),
            in_specs=[
                pl.BlockSpec((act.shape[0], part_rows * cap), lambda i, o, t: (0, i)),
                pl.BlockSpec(down.shape, lambda i, o, t: (0, 0)),
                pl.BlockSpec((None, part_rows, cap, width), lambda i, o, t: (t[0], i, 0, 0)),
            ],
            out_specs=pl.BlockSpec((sources, cap, width), lambda i, o, t: (0, 0, 0)),
        ),
        out_shape=jax.ShapeDtypeStruct((sources, cap, width), jnp.bfloat16),
        name="expert_out",
    )(order, tp, act, down, full)


def give_back_kernel(eps, send_ref, came_ref, own_sem, send_sem, recv_sem):
    ep = lax.axis_index("ep")
    barrier = pltpu.get_barrier_semaphore()

    def greet(k, carry):
        pl.semaphore_signal(
            barrier, inc=1, device_id={"ep": lax.rem(ep + k, eps)}, device_id_type=MESH
        )
        return carry

    lax.fori_loop(1, eps, greet, 0)
    own = pltpu.make_async_copy(send_ref.at[ep], came_ref.at[ep], own_sem)
    own.start()
    pl.semaphore_wait(barrier, eps - 1)

    def post(k, carry):
        dst = lax.rem(ep + lax.rem(k * STRIDE, eps), eps)
        pltpu.make_async_remote_copy(
            src_ref=send_ref.at[dst],
            dst_ref=came_ref.at[ep],
            send_sem=send_sem,
            recv_sem=recv_sem,
            device_id={"ep": dst},
            device_id_type=MESH,
        ).start()
        return carry

    lax.fori_loop(1, eps, post, 0)
    own.wait()
    most = send_ref.at[pl.ds(0, eps - 1)]
    pltpu.make_async_copy(most, most, send_sem).wait()
    pltpu.make_async_copy(most, most, recv_sem).wait()


def give_back(send, eps):
    dma = pltpu.SemaphoreType.DMA
    return pl.pallas_call(
        functools.partial(give_back_kernel, eps),
        out_shape=jax.ShapeDtypeStruct(send.shape, send.dtype),
        in_specs=[pl.BlockSpec(memory_space=pl.ANY)],
        out_specs=pl.BlockSpec(memory_space=pl.ANY),
        scratch_shapes=[dma, dma, dma],
        compiler_params=pltpu.CompilerParams(collective_id=3, has_side_effects=True),
        name="give_back",
    )(send)


def combine_kernel(experts_ref, mix_ref, came_ref, out_ref):
    count, cap, width = came_ref.shape
    _, weighted = slot_matrices(experts_ref[...], mix_ref[...], count)
    rows = came_ref[...].astype(jnp.float32).reshape(count * cap, width).astype(jnp.bfloat16)
    out_ref[...] = jnp.dot(weighted, rows, preferred_element_type=jnp.float32).astype(jnp.bfloat16)


def combine(experts, mix, came):
    return pl.pallas_call(
        combine_kernel,
        out_shape=jax.ShapeDtypeStruct((experts.shape[0], came.shape[2]), jnp.bfloat16),
        name="combine",
    )(experts, mix, came)


def shards(
    queries,
    new_keys,
    new_values,
    key_cache,
    value_cache,
    cache_lengths,
    request_order,
    residual,
    out_weight,
    norm_gain,
    route_experts,
    route_weights,
    expert_gate,
    expert_up,
    expert_down,
):
    tps = lax.axis_size("tp")
    eps = lax.axis_size("ep")
    ep = lax.axis_index("ep")
    tp = lax.axis_index("tp")
    context = attention_block(
        queries, new_keys, new_values, key_cache, value_cache, cache_lengths, KVHEADS // tps
    )
    head_terms = jnp.dot(context, out_weight, preferred_element_type=jnp.float32)
    terms = exchange(head_terms.astype(jnp.bfloat16), tps)
    tokens, top = route_experts.shape
    mixing = (route_weights / jnp.sum(route_weights, axis=1, keepdims=True)).astype(jnp.bfloat16)
    meta = jnp.concatenate(
        [route_experts.astype(jnp.bfloat16).reshape(-1), mixing.reshape(-1)]
    )
    pairs = tokens * top
    meta = jnp.pad(meta, (0, -(2 * pairs) % 1024)).reshape(-1, 128)
    send = prepare(terms, residual, route_experts, eps)
    full, metas = dispatch(send, meta, eps, tps)
    act = expert_in(full, norm_gain[None, :], expert_gate[0], expert_up[0])
    act_full = gather(act, tps).reshape(-1, act.shape[1])
    back = expert_out(request_order, act_full, expert_down[0], full, tp[None].astype(jnp.int32))
    came = give_back(back, eps)
    origin = jnp.argmax(request_order == ep).astype(jnp.int32)
    theirs = lax.dynamic_index_in_dim(metas, origin, 0, keepdims=False).reshape(-1)
    their_experts = theirs[:pairs].reshape(tokens, top).astype(jnp.int32)
    their_mix = theirs[pairs : 2 * pairs].reshape(tokens, top).astype(jnp.float32)
    return combine(their_experts, their_mix, came)


def solution(mesh):
    return jax.shard_map(
        shards,
        mesh=mesh,
        in_specs=(
            P("ep", "tp"),
            P("ep", "tp"),
            P("ep", "tp"),
            P("ep", None, "tp"),
            P("ep", None, "tp"),
            P("ep"),
            P(),
            P("ep", "tp"),
            P("tp", None),
            P(),
            P("ep", None),
            P("ep", None),
            P("ep", None, "tp"),
            P("ep", None, "tp"),
            P("ep", None, "tp"),
        ),
        out_specs=P("ep", "tp"),
        check_vma=False,
    )
```

```python
import functools
import math

import jax
import jax.numpy as jnp
from jax import lax
from jax.experimental import pallas as pl
from jax.experimental.pallas import tpu as pltpu
from jax.sharding import PartitionSpec as P

HEAD = 128
QHEADS = 16
KVHEADS = 4
CAP = 8
STRIDE = 37
LAG = 32
AHEAD = 48
MESH = pl.DeviceIdType.MESH


def attention_block(queries, new_keys, new_values, key_cache, value_cache, cache_lengths, kv_local):
    tokens_here = queries.shape[0]
    cached = key_cache.shape[1]
    group_size = QHEADS // KVHEADS
    query_view = queries.reshape(tokens_here, kv_local, group_size, HEAD)
    all_keys = jnp.concatenate([key_cache[0], new_keys], axis=0).reshape(
        cached + tokens_here, kv_local, HEAD
    )
    all_values = jnp.concatenate([value_cache[0], new_values], axis=0).reshape(
        cached + tokens_here, kv_local, HEAD
    )
    scores = jnp.einsum(
        "tghd,kgd->tghk", query_view, all_keys, preferred_element_type=jnp.float32
    ) / math.sqrt(HEAD)
    position = jnp.arange(cached + tokens_here, dtype=jnp.int32)
    current = jnp.arange(tokens_here, dtype=jnp.int32)
    visible = jnp.where(
        position[None, :] < cached,
        position[None, :] < cache_lengths[0],
        position[None, :] - cached <= current[:, None],
    )
    visible = visible[:, None, None, :]
    highest = jnp.max(jnp.where(visible, scores, -1e30), axis=-1, keepdims=True)
    raised = jnp.exp(jnp.where(visible, scores - highest, -1e30))
    totals = jnp.sum(raised, axis=-1, keepdims=True)
    weights = raised.astype(jnp.bfloat16)
    context = (
        jnp.einsum("tghk,kgd->tghd", weights, all_values, preferred_element_type=jnp.float32)
        / totals
    )
    return context.astype(jnp.bfloat16).reshape(tokens_here, -1)


def row_span(eps):
    return 16 if eps > 16 else 2


def exchange_kernel(tps, x_ref, out_ref, send_sem, recv_sem, own_sem):
    tp = lax.axis_index("tp")
    width = out_ref.shape[2]
    barrier = pltpu.get_barrier_semaphore()
    for o in range(1, tps):
        pl.semaphore_signal(
            barrier, inc=1, device_id={"tp": lax.rem(tp + o, tps)}, device_id_type=MESH
        )
    own = pltpu.make_async_copy(
        x_ref.at[:, pl.ds(pl.multiple_of(tp * width, width), width)], out_ref.at[0], own_sem
    )
    own.start()
    pl.semaphore_wait(barrier, tps - 1)
    copies = []
    for o in range(1, tps):
        peer = lax.rem(tp + o, tps)
        copy = pltpu.make_async_remote_copy(
            src_ref=x_ref.at[:, pl.ds(pl.multiple_of(peer * width, width), width)],
            dst_ref=out_ref.at[o],
            send_sem=send_sem.at[o - 1],
            recv_sem=recv_sem.at[o - 1],
            device_id={"tp": peer},
            device_id_type=MESH,
        )
        copy.start()
        copies.append(copy)
    own.wait()
    for copy in copies:
        copy.wait()


def exchange(terms, tps):
    rows, total = terms.shape
    return pl.pallas_call(
        functools.partial(exchange_kernel, tps),
        out_shape=jax.ShapeDtypeStruct((tps, rows, total // tps), terms.dtype),
        in_specs=[pl.BlockSpec(memory_space=pltpu.VMEM)],
        out_specs=pl.BlockSpec(memory_space=pltpu.VMEM),
        scratch_shapes=[
            pltpu.SemaphoreType.DMA((tps - 1,)),
            pltpu.SemaphoreType.DMA((tps - 1,)),
            pltpu.SemaphoreType.DMA,
        ],
        compiler_params=pltpu.CompilerParams(collective_id=0, has_side_effects=True),
        name="tp_exchange",
    )(terms)


def slot_matrices(experts, mix, count):
    tokens, top = experts.shape
    lanes = lax.broadcasted_iota(jnp.int32, (tokens, count), 1)
    named = jnp.zeros((tokens, count), jnp.float32)
    mixed = jnp.zeros((tokens, count), jnp.float32)
    for k in range(top):
        hit = experts[:, k : k + 1] == lanes
        named = jnp.where(hit, 1.0, named)
        mixed = jnp.where(hit, mix[:, k : k + 1], mixed)
    row = lax.broadcasted_iota(jnp.int32, (tokens, tokens), 0)
    col = lax.broadcasted_iota(jnp.int32, (tokens, tokens), 1)
    earlier = jnp.where(col < row, 1.0, 0.0).astype(jnp.bfloat16)
    rank = jnp.dot(earlier, named.astype(jnp.bfloat16), preferred_element_type=jnp.float32)
    marked = jnp.where(named > 0.0, rank, 255.0).astype(jnp.bfloat16)
    source = lax.broadcasted_iota(jnp.int32, (count, count * CAP), 0)
    target = lax.broadcasted_iota(jnp.int32, (count, count * CAP), 1)
    spread = jnp.where(target // CAP == source, 1.0, 0.0).astype(jnp.bfloat16)
    rank_wide = jnp.dot(marked, spread, preferred_element_type=jnp.float32)
    mix_wide = jnp.dot(mixed.astype(jnp.bfloat16), spread, preferred_element_type=jnp.float32)
    place = lax.rem(
        lax.broadcasted_iota(jnp.int32, (tokens, count * CAP), 1), CAP
    ).astype(jnp.float32)
    chosen = rank_wide == place
    selector = jnp.where(chosen, 1.0, 0.0).astype(jnp.bfloat16)
    weighted = jnp.where(chosen, mix_wide, 0.0).astype(jnp.bfloat16)
    return selector, weighted


def prepare_kernel(count, terms_ref, residual_ref, experts_ref, out_ref):
    total = residual_ref[...].astype(jnp.float32)
    for o in range(terms_ref.shape[0]):
        total = total + terms_ref[o].astype(jnp.float32)
    hidden = total.astype(jnp.bfloat16)
    experts = experts_ref[...]
    selector, _ = slot_matrices(experts, experts.astype(jnp.float32), count)
    rows = lax.dot_general(
        selector, hidden, (((0,), (0,)), ((), ())), preferred_element_type=jnp.float32
    )
    out_ref[...] = rows.reshape(out_ref.shape).astype(jnp.bfloat16)


def prepare(terms, residual, experts, count):
    return pl.pallas_call(
        functools.partial(prepare_kernel, count),
        out_shape=jax.ShapeDtypeStruct((count, CAP, residual.shape[1]), jnp.bfloat16),
        name="prepare",
    )(terms, residual, experts)


def dispatch_kernel(
    eps,
    tps,
    send_ref,
    meta_ref,
    full_ref,
    metas_ref,
    own_sem,
    send_sem,
    meta_send,
    meta_recv,
    recv_sem,
    right_send,
    left_send,
    left_recv,
    right_recv,
    relay_send,
    relay_recv,
):
    ep = lax.axis_index("ep")
    tp = lax.axis_index("tp")
    right = lax.rem(tp + 1, tps)
    left = lax.rem(tp + tps - 1, tps)
    barrier = pltpu.get_barrier_semaphore()

    def greet(k, carry):
        pl.semaphore_signal(
            barrier, inc=1, device_id={"ep": lax.rem(ep + k, eps)}, device_id_type=MESH
        )
        return carry

    for side in (right, left):
        pl.semaphore_signal(barrier, inc=1, device_id={"tp": side}, device_id_type=MESH)
    lax.fori_loop(1, eps, greet, 0)
    own = pltpu.make_async_copy(send_ref.at[ep], full_ref.at[tp, ep], recv_sem.at[0])
    own.start()
    own_meta = pltpu.make_async_copy(meta_ref, metas_ref.at[ep], own_sem)
    own_meta.start()
    span = row_span(eps)
    rows = eps // span
    row = lax.div(ep, span)
    place = lax.rem(ep, span)
    pl.semaphore_wait(barrier, eps + 1)

    def offset(k):
        return lax.rem(k * STRIDE, eps)

    def source(k):
        return lax.rem(ep + eps - offset(k), eps)

    def post(k):
        off = offset(k)
        dst = lax.rem(ep + off, eps)
        pltpu.make_async_remote_copy(
            src_ref=send_ref.at[dst],
            dst_ref=full_ref.at[tp, ep],
            send_sem=send_sem,
            recv_sem=recv_sem.at[off],
            device_id={"ep": dst},
            device_id_type=MESH,
        ).start()

    def meta_near(k, carry):
        pltpu.make_async_remote_copy(
            src_ref=meta_ref,
            dst_ref=metas_ref.at[ep],
            send_sem=meta_send.at[0],
            recv_sem=meta_recv.at[0],
            device_id={"ep": row * span + lax.rem(place + k, span)},
            device_id_type=MESH,
        ).start()
        return carry

    def meta_far(k, carry):
        ours = metas_ref.at[pl.ds(row * span, span)]
        pltpu.make_async_remote_copy(
            src_ref=ours,
            dst_ref=ours,
            send_sem=meta_send.at[1],
            recv_sem=meta_recv.at[1],
            device_id={"ep": lax.rem(row + k, rows) * span + place},
            device_id_type=MESH,
        ).start()
        return carry

    def spread(k):
        block = full_ref.at[tp, source(k)]
        pltpu.make_async_copy(block, block, recv_sem.at[offset(k)]).wait()
        for side, ssem, rsem in ((right, right_send, left_recv), (left, left_send, right_recv)):
            pltpu.make_async_remote_copy(
                src_ref=block,
                dst_ref=block,
                send_sem=ssem,
                recv_sem=rsem.at[k],
                device_id={"tp": side},
                device_id_type=MESH,
            ).start()

    def relay(k, way):
        src = source(k)
        from_left = full_ref.at[left, src]
        from_right = full_ref.at[right, src]
        pltpu.make_async_copy(from_left, from_left, left_recv.at[k]).wait()
        pltpu.make_async_copy(from_right, from_right, right_recv.at[k]).wait()
        block, side = ((from_left, right), (from_right, left))[way]
        pltpu.make_async_remote_copy(
            src_ref=block,
            dst_ref=block,
            send_sem=relay_send.at[way],
            recv_sem=relay_recv.at[way],
            device_id={"tp": side},
            device_id_type=MESH,
        ).start()

    def drain(ref, sem):
        pltpu.make_async_copy(ref, ref, sem).wait()

    def pairs(low, high, step):
        def both(i, carry):
            for way in range(2):
                step(2 * i + way, way)
            return carry

        lax.fori_loop(low // 2, high // 2, both, 0)

    def first(k, carry):
        post(k)
        return carry

    def opening(k, way):
        post(k + ahead)
        spread(k)

    def middle(k, way):
        post(k + ahead)
        spread(k)
        relay(k - lag, way)

    def closing(k, way):
        spread(k)
        relay(k - lag, way)

    ahead, lag = min(AHEAD, eps // 2), min(LAG, eps // 2)
    lax.fori_loop(1, ahead, first, 0)
    lax.fori_loop(1, span, meta_near, 0)
    pairs(0, lag, opening)
    pairs(lag, eps - ahead, middle)
    own_meta.wait()
    near = metas_ref.at[pl.ds(0, span - 1)]
    drain(near, meta_recv.at[0])
    lax.fori_loop(1, rows, meta_far, 0)
    pairs(eps - ahead, eps, closing)
    pairs(eps - lag, eps, relay)
    drain(near, meta_send.at[0])
    far = metas_ref.at[pl.ds(0, (rows - 1) * span)]
    drain(far, meta_send.at[1])
    drain(far, meta_recv.at[1])
    drain(send_ref.at[pl.ds(0, eps - 1)], send_sem)
    drain(send_ref, right_send)
    drain(send_ref, left_send)
    half = send_ref.at[pl.ds(0, eps // 2)]
    for way in range(2):
        drain(half, relay_send.at[way])
        drain(half, relay_recv.at[way])


def dispatch(send, meta, eps, tps):
    dma = pltpu.SemaphoreType.DMA
    return pl.pallas_call(
        functools.partial(dispatch_kernel, eps, tps),
        out_shape=(
            jax.ShapeDtypeStruct((tps,) + send.shape, send.dtype),
            jax.ShapeDtypeStruct((eps,) + meta.shape, meta.dtype),
        ),
        in_specs=[pl.BlockSpec(memory_space=pl.ANY)] * 2,
        out_specs=(pl.BlockSpec(memory_space=pl.ANY),) * 2,
        scratch_shapes=[
            dma, dma, dma((2,)), dma((2,)), dma((eps,)), dma, dma, dma((eps,)), dma((eps,)), dma((2,)), dma((2,))
        ],
        compiler_params=pltpu.CompilerParams(collective_id=1, has_side_effects=True),
        name="dispatch",
    )(send, meta)


def expert_in_kernel(rows_ref, gain_ref, gate_ref, up_ref, out_ref):
    parts, sources, cap, width = rows_ref.shape
    rows = sources * cap
    total = parts * width
    wide = [rows_ref[p].astype(jnp.float32).reshape(rows, width) for p in range(parts)]
    squares = sum(jnp.sum(part * part, axis=1, keepdims=True) for part in wide)
    factor = lax.rsqrt(squares / total + 1e-06)
    normed = jnp.concatenate(
        [
            (part * factor * gain_ref[:, p * width : (p + 1) * width]).astype(jnp.bfloat16)
            for p, part in enumerate(wide)
        ],
        axis=1,
    )
    dims = (((1,), (1,)), ((), ()))
    gate = lax.dot_general(gate_ref[...], normed, dims, preferred_element_type=jnp.float32)
    up = lax.dot_general(up_ref[...], normed, dims, preferred_element_type=jnp.float32)
    out_ref[...] = (gate / (1.0 + jnp.exp(-gate)) * up).astype(jnp.bfloat16)


def expert_in(full, gain, gate, up):
    parts, sources, cap, width = full.shape
    tiles = 4 if sources >= 64 else 1
    part_rows = sources // tiles
    ff = gate.shape[0]
    return pl.pallas_call(
        expert_in_kernel,
        grid=(tiles,),
        out_shape=jax.ShapeDtypeStruct((ff, sources * cap), jnp.bfloat16),
        in_specs=[
            pl.BlockSpec((parts, part_rows, cap, width), lambda i: (0, i, 0, 0)),
            pl.BlockSpec((1, gain.shape[1]), lambda i: (0, 0)),
            pl.BlockSpec(gate.shape, lambda i: (0, 0)),
            pl.BlockSpec(up.shape, lambda i: (0, 0)),
        ],
        out_specs=pl.BlockSpec((ff, part_rows * cap), lambda i: (0, i)),
        name="expert_in",
    )(full, gain, gate, up)


def gather_kernel(tps, chunks, x_ref, out_ref, own_sem, send_sem, recv_sem, relay_send, relay_recv):
    tp = lax.axis_index("tp")
    right = lax.rem(tp + 1, tps)
    left = lax.rem(tp + tps - 1, tps)
    sides = (right, left)
    barrier = pltpu.get_barrier_semaphore()
    for side in sides:
        pl.semaphore_signal(barrier, inc=1, device_id={"tp": side}, device_id_type=MESH)
    own = pltpu.make_async_copy(x_ref, out_ref.at[tp], own_sem)
    own.start()
    pl.semaphore_wait(barrier, 2)
    size = x_ref.shape[0] // chunks
    copies = []
    for c in range(chunks):
        part = pl.ds(c * size, size)
        pair = []
        for way in range(2):
            copy = pltpu.make_async_remote_copy(
                src_ref=x_ref.at[part],
                dst_ref=out_ref.at[tp, part],
                send_sem=send_sem.at[way, c],
                recv_sem=recv_sem.at[way, c],
                device_id={"tp": sides[way]},
                device_id_type=MESH,
            )
            copy.start()
            pair.append(copy)
        copies.append(pair)
    relays = []
    for c in range(chunks):
        part = pl.ds(c * size, size)
        way = c % 2
        for pair in copies[c]:
            pair.wait_recv()
        block = out_ref.at[(left, right)[way], part]
        copy = pltpu.make_async_remote_copy(
            src_ref=block,
            dst_ref=block,
            send_sem=relay_send.at[c],
            recv_sem=relay_recv.at[c],
            device_id={"tp": sides[way]},
            device_id_type=MESH,
        )
        copy.start()
        relays.append(copy)
    own.wait()
    for pair in copies:
        for copy in pair:
            copy.wait_send()
    for copy in relays:
        copy.wait()


def gather(x, tps):
    chunks = 4 if x.shape[0] % 64 == 0 else 2
    dma = pltpu.SemaphoreType.DMA
    return pl.pallas_call(
        functools.partial(gather_kernel, tps, chunks),
        out_shape=jax.ShapeDtypeStruct((tps,) + x.shape, x.dtype),
        in_specs=[pl.BlockSpec(memory_space=pltpu.VMEM)],
        out_specs=pl.BlockSpec(memory_space=pltpu.VMEM),
        scratch_shapes=[dma, dma((2, chunks)), dma((2, chunks)), dma((chunks,)), dma((chunks,))],
        compiler_params=pltpu.CompilerParams(collective_id=2, has_side_effects=True),
        name="tp_gather",
    )(x)


def expert_out_kernel(order_ref, act_ref, down_ref, own_ref, out_ref):
    sources, cap, width = own_ref.shape
    base = pl.program_id(0) * sources
    value = lax.dot_general(
        act_ref[...], down_ref[...], (((0,), (0,)), ((), ())), preferred_element_type=jnp.float32
    )
    value = value.reshape(sources, cap, width) + own_ref[...].astype(jnp.float32)
    value = value.astype(jnp.bfloat16)
    for j in range(sources):
        out_ref[order_ref[base + j]] = value[j]


def expert_out(order, act, down, full, tp):
    parts, sources, cap, width = full.shape
    tiles = 4 if sources >= 64 else 1
    part_rows = sources // tiles
    return pl.pallas_call(
        lambda order_ref, tp_ref, act_ref, down_ref, own_ref, out_ref: expert_out_kernel(
            order_ref, act_ref, down_ref, own_ref, out_ref
        ),
        grid_spec=pltpu.PrefetchScalarGridSpec(
            num_scalar_prefetch=2,
            grid=(tiles,),
            in_specs=[
                pl.BlockSpec((act.shape[0], part_rows * cap), lambda i, o, t: (0, i)),
                pl.BlockSpec(down.shape, lambda i, o, t: (0, 0)),
                pl.BlockSpec((None, part_rows, cap, width), lambda i, o, t: (t[0], i, 0, 0)),
            ],
            out_specs=pl.BlockSpec((sources, cap, width), lambda i, o, t: (0, 0, 0)),
        ),
        out_shape=jax.ShapeDtypeStruct((sources, cap, width), jnp.bfloat16),
        name="expert_out",
    )(order, tp, act, down, full)


def give_back_kernel(eps, send_ref, came_ref, own_sem, send_sem, recv_sem):
    ep = lax.axis_index("ep")
    barrier = pltpu.get_barrier_semaphore()

    def greet(k, carry):
        pl.semaphore_signal(
            barrier, inc=1, device_id={"ep": lax.rem(ep + k, eps)}, device_id_type=MESH
        )
        return carry

    lax.fori_loop(1, eps, greet, 0)
    own = pltpu.make_async_copy(send_ref.at[ep], came_ref.at[ep], own_sem)
    own.start()
    pl.semaphore_wait(barrier, eps - 1)

    def post(k, carry):
        dst = lax.rem(ep + lax.rem(k * STRIDE, eps), eps)
        pltpu.make_async_remote_copy(
            src_ref=send_ref.at[dst],
            dst_ref=came_ref.at[ep],
            send_sem=send_sem,
            recv_sem=recv_sem,
            device_id={"ep": dst},
            device_id_type=MESH,
        ).start()
        return carry

    lax.fori_loop(1, eps, post, 0)
    own.wait()
    most = send_ref.at[pl.ds(0, eps - 1)]
    pltpu.make_async_copy(most, most, send_sem).wait()
    pltpu.make_async_copy(most, most, recv_sem).wait()


def give_back(send, eps):
    dma = pltpu.SemaphoreType.DMA
    return pl.pallas_call(
        functools.partial(give_back_kernel, eps),
        out_shape=jax.ShapeDtypeStruct(send.shape, send.dtype),
        in_specs=[pl.BlockSpec(memory_space=pl.ANY)],
        out_specs=pl.BlockSpec(memory_space=pl.ANY),
        scratch_shapes=[dma, dma, dma],
        compiler_params=pltpu.CompilerParams(collective_id=3, has_side_effects=True),
        name="give_back",
    )(send)


def combine_kernel(experts_ref, mix_ref, came_ref, out_ref):
    count, cap, width = came_ref.shape
    _, weighted = slot_matrices(experts_ref[...], mix_ref[...], count)
    rows = came_ref[...].astype(jnp.float32).reshape(count * cap, width).astype(jnp.bfloat16)
    out_ref[...] = jnp.dot(weighted, rows, preferred_element_type=jnp.float32).astype(jnp.bfloat16)


def combine(experts, mix, came):
    return pl.pallas_call(
        combine_kernel,
        out_shape=jax.ShapeDtypeStruct((experts.shape[0], came.shape[2]), jnp.bfloat16),
        name="combine",
    )(experts, mix, came)


def shards(
    queries,
    new_keys,
    new_values,
    key_cache,
    value_cache,
    cache_lengths,
    request_order,
    residual,
    out_weight,
    norm_gain,
    route_experts,
    route_weights,
    expert_gate,
    expert_up,
    expert_down,
):
    tps = lax.axis_size("tp")
    eps = lax.axis_size("ep")
    ep = lax.axis_index("ep")
    tp = lax.axis_index("tp")
    context = attention_block(
        queries, new_keys, new_values, key_cache, value_cache, cache_lengths, KVHEADS // tps
    )
    head_terms = jnp.dot(context, out_weight, preferred_element_type=jnp.float32)
    terms = exchange(head_terms.astype(jnp.bfloat16), tps)
    tokens, top = route_experts.shape
    mixing = (route_weights / jnp.sum(route_weights, axis=1, keepdims=True)).astype(jnp.bfloat16)
    meta = jnp.concatenate(
        [route_experts.astype(jnp.bfloat16).reshape(-1), mixing.reshape(-1)]
    )
    pairs = tokens * top
    meta = jnp.pad(meta, (0, -(2 * pairs) % 1024)).reshape(-1, 128)
    send = prepare(terms, residual, route_experts, eps)
    full, metas = dispatch(send, meta, eps, tps)
    act = expert_in(full, norm_gain[None, :], expert_gate[0].T, expert_up[0].T)
    act_full = gather(act, tps).reshape(-1, act.shape[1])
    back = expert_out(request_order, act_full, expert_down[0], full, tp[None].astype(jnp.int32))
    came = give_back(back, eps)
    origin = jnp.argmax(request_order == ep).astype(jnp.int32)
    theirs = lax.dynamic_index_in_dim(metas, origin, 0, keepdims=False).reshape(-1)
    their_experts = theirs[:pairs].reshape(tokens, top).astype(jnp.int32)
    their_mix = theirs[pairs : 2 * pairs].reshape(tokens, top).astype(jnp.float32)
    return combine(their_experts, their_mix, came)


def solution(mesh):
    return jax.shard_map(
        shards,
        mesh=mesh,
        in_specs=(
            P("ep", "tp"),
            P("ep", "tp"),
            P("ep", "tp"),
            P("ep", None, "tp"),
            P("ep", None, "tp"),
            P("ep"),
            P(),
            P("ep", "tp"),
            P("tp", None),
            P(),
            P("ep", None),
            P("ep", None),
            P("ep", None, "tp"),
            P("ep", None, "tp"),
            P("ep", None, "tp"),
        ),
        out_specs=P("ep", "tp"),
        check_vma=False,
    )
```

```python
import functools
import math

import jax
import jax.numpy as jnp
from jax import lax
from jax.experimental import pallas as pl
from jax.experimental.pallas import tpu as pltpu
from jax.sharding import PartitionSpec as P

HEAD = 128
QHEADS = 16
KVHEADS = 4
CAP = 8
STRIDE = 37
LAG = 32
AHEAD = 48
MESH = pl.DeviceIdType.MESH


def attention_block(queries, new_keys, new_values, key_cache, value_cache, cache_lengths, kv_local):
    tokens_here = queries.shape[0]
    cached = key_cache.shape[1]
    group_size = QHEADS // KVHEADS
    query_view = queries.reshape(tokens_here, kv_local, group_size, HEAD)
    all_keys = jnp.concatenate([key_cache[0], new_keys], axis=0).reshape(
        cached + tokens_here, kv_local, HEAD
    )
    all_values = jnp.concatenate([value_cache[0], new_values], axis=0).reshape(
        cached + tokens_here, kv_local, HEAD
    )
    scores = jnp.einsum(
        "tghd,kgd->tghk", query_view, all_keys, preferred_element_type=jnp.float32
    ) / math.sqrt(HEAD)
    position = jnp.arange(cached + tokens_here, dtype=jnp.int32)
    current = jnp.arange(tokens_here, dtype=jnp.int32)
    visible = jnp.where(
        position[None, :] < cached,
        position[None, :] < cache_lengths[0],
        position[None, :] - cached <= current[:, None],
    )
    visible = visible[:, None, None, :]
    highest = jnp.max(jnp.where(visible, scores, -1e30), axis=-1, keepdims=True)
    raised = jnp.exp(jnp.where(visible, scores - highest, -1e30))
    totals = jnp.sum(raised, axis=-1, keepdims=True)
    weights = raised.astype(jnp.bfloat16)
    context = (
        jnp.einsum("tghk,kgd->tghd", weights, all_values, preferred_element_type=jnp.float32)
        / totals
    )
    return context.astype(jnp.bfloat16).reshape(tokens_here, -1)


def row_span(eps):
    return 16 if eps > 16 else 2


def exchange_kernel(tps, x_ref, out_ref, send_sem, recv_sem, own_sem):
    tp = lax.axis_index("tp")
    width = out_ref.shape[2]
    barrier = pltpu.get_barrier_semaphore()
    for o in range(1, tps):
        pl.semaphore_signal(
            barrier, inc=1, device_id={"tp": lax.rem(tp + o, tps)}, device_id_type=MESH
        )
    own = pltpu.make_async_copy(
        x_ref.at[:, pl.ds(pl.multiple_of(tp * width, width), width)], out_ref.at[0], own_sem
    )
    own.start()
    pl.semaphore_wait(barrier, tps - 1)
    copies = []
    for o in range(1, tps):
        peer = lax.rem(tp + o, tps)
        copy = pltpu.make_async_remote_copy(
            src_ref=x_ref.at[:, pl.ds(pl.multiple_of(peer * width, width), width)],
            dst_ref=out_ref.at[o],
            send_sem=send_sem.at[o - 1],
            recv_sem=recv_sem.at[o - 1],
            device_id={"tp": peer},
            device_id_type=MESH,
        )
        copy.start()
        copies.append(copy)
    own.wait()
    for copy in copies:
        copy.wait()


def exchange(terms, tps):
    rows, total = terms.shape
    return pl.pallas_call(
        functools.partial(exchange_kernel, tps),
        out_shape=jax.ShapeDtypeStruct((tps, rows, total // tps), terms.dtype),
        in_specs=[pl.BlockSpec(memory_space=pltpu.VMEM)],
        out_specs=pl.BlockSpec(memory_space=pltpu.VMEM),
        scratch_shapes=[
            pltpu.SemaphoreType.DMA((tps - 1,)),
            pltpu.SemaphoreType.DMA((tps - 1,)),
            pltpu.SemaphoreType.DMA,
        ],
        compiler_params=pltpu.CompilerParams(collective_id=0, has_side_effects=True),
        name="tp_exchange",
    )(terms)


def slot_matrices(experts, mix, count):
    top, tokens = experts.shape
    number = lax.broadcasted_iota(jnp.int32, (count, tokens), 0).astype(jnp.float32)
    named = jnp.zeros((count, tokens), jnp.float32)
    mixed = jnp.zeros((count, tokens), jnp.float32)
    for k in range(top):
        hit = experts[k : k + 1, :] == number
        named = jnp.where(hit, 1.0, named)
        mixed = jnp.where(hit, mix[k : k + 1, :], mixed)
    row = lax.broadcasted_iota(jnp.int32, (tokens, tokens), 0)
    col = lax.broadcasted_iota(jnp.int32, (tokens, tokens), 1)
    earlier = jnp.where(row < col, 1.0, 0.0).astype(jnp.bfloat16)
    rank = jnp.dot(named.astype(jnp.bfloat16), earlier, preferred_element_type=jnp.float32)
    marked = jnp.where(named > 0.0, rank, 255.0).astype(jnp.bfloat16)
    target = lax.broadcasted_iota(jnp.int32, (count * CAP, count), 0)
    source = lax.broadcasted_iota(jnp.int32, (count * CAP, count), 1)
    spread = jnp.where(target // CAP == source, 1.0, 0.0).astype(jnp.bfloat16)
    rank_wide = jnp.dot(spread, marked, preferred_element_type=jnp.float32)
    mix_wide = jnp.dot(spread, mixed.astype(jnp.bfloat16), preferred_element_type=jnp.float32)
    place = lax.rem(
        lax.broadcasted_iota(jnp.int32, (count * CAP, tokens), 0), CAP
    ).astype(jnp.float32)
    chosen = rank_wide == place
    selector = jnp.where(chosen, 1.0, 0.0).astype(jnp.bfloat16)
    weighted = jnp.where(chosen, mix_wide, 0.0).astype(jnp.bfloat16)
    return selector, weighted


def prepare_kernel(count, terms_ref, residual_ref, experts_ref, weights_ref, out_ref, meta_ref):
    total = residual_ref[...].astype(jnp.float32)
    for o in range(terms_ref.shape[0]):
        total = total + terms_ref[o].astype(jnp.float32)
    hidden = total.astype(jnp.bfloat16)
    experts = experts_ref[...].astype(jnp.float32)
    weights = weights_ref[...]
    mix = weights / jnp.sum(weights, axis=0, keepdims=True)
    selector, _ = slot_matrices(experts, mix, count)
    rows = jnp.dot(selector, hidden, preferred_element_type=jnp.float32)
    out_ref[...] = rows.reshape(out_ref.shape).astype(jnp.bfloat16)
    meta_ref[...] = jnp.zeros_like(meta_ref)
    meta_ref[:, : experts.shape[1]] = jnp.concatenate([experts, mix], axis=0).astype(jnp.bfloat16)


def prepare(terms, residual, experts, weights, count):
    return pl.pallas_call(
        functools.partial(prepare_kernel, count),
        out_shape=(
            jax.ShapeDtypeStruct((count, CAP, residual.shape[1]), jnp.bfloat16),
            jax.ShapeDtypeStruct((2 * experts.shape[0], 128), jnp.bfloat16),
        ),
        name="prepare",
    )(terms, residual, experts, weights)


def dispatch_kernel(
    eps,
    tps,
    send_ref,
    meta_ref,
    full_ref,
    metas_ref,
    own_sem,
    send_sem,
    meta_send,
    meta_recv,
    recv_sem,
    right_send,
    left_send,
    left_recv,
    right_recv,
    relay_send,
    relay_recv,
):
    ep = lax.axis_index("ep")
    tp = lax.axis_index("tp")
    right = lax.rem(tp + 1, tps)
    left = lax.rem(tp + tps - 1, tps)
    barrier = pltpu.get_barrier_semaphore()

    def greet(k, carry):
        pl.semaphore_signal(
            barrier, inc=1, device_id={"ep": lax.rem(ep + k, eps)}, device_id_type=MESH
        )
        return carry

    for side in (right, left):
        pl.semaphore_signal(barrier, inc=1, device_id={"tp": side}, device_id_type=MESH)
    lax.fori_loop(1, eps, greet, 0)
    own = pltpu.make_async_copy(send_ref.at[ep], full_ref.at[tp, ep], recv_sem.at[0])
    own.start()
    own_meta = pltpu.make_async_copy(meta_ref, metas_ref.at[ep], own_sem)
    own_meta.start()
    span = row_span(eps)
    rows = eps // span
    row = lax.div(ep, span)
    place = lax.rem(ep, span)
    pl.semaphore_wait(barrier, eps + 1)

    def offset(k):
        return lax.rem(k * STRIDE, eps)

    def source(k):
        return lax.rem(ep + eps - offset(k), eps)

    def post(k):
        off = offset(k)
        dst = lax.rem(ep + off, eps)
        pltpu.make_async_remote_copy(
            src_ref=send_ref.at[dst],
            dst_ref=full_ref.at[tp, ep],
            send_sem=send_sem,
            recv_sem=recv_sem.at[off],
            device_id={"ep": dst},
            device_id_type=MESH,
        ).start()

    def meta_near(k, carry):
        pltpu.make_async_remote_copy(
            src_ref=meta_ref,
            dst_ref=metas_ref.at[ep],
            send_sem=meta_send.at[0],
            recv_sem=meta_recv.at[0],
            device_id={"ep": row * span + lax.rem(place + k, span)},
            device_id_type=MESH,
        ).start()
        return carry

    def meta_far(k, carry):
        ours = metas_ref.at[pl.ds(row * span, span)]
        pltpu.make_async_remote_copy(
            src_ref=ours,
            dst_ref=ours,
            send_sem=meta_send.at[1],
            recv_sem=meta_recv.at[1],
            device_id={"ep": lax.rem(row + k, rows) * span + place},
            device_id_type=MESH,
        ).start()
        return carry

    def spread(k):
        block = full_ref.at[tp, source(k)]
        pltpu.make_async_copy(block, block, recv_sem.at[offset(k)]).wait()
        for side, ssem, rsem in ((right, right_send, left_recv), (left, left_send, right_recv)):
            pltpu.make_async_remote_copy(
                src_ref=block,
                dst_ref=block,
                send_sem=ssem,
                recv_sem=rsem.at[k],
                device_id={"tp": side},
                device_id_type=MESH,
            ).start()

    def relay(k, way):
        src = source(k)
        from_left = full_ref.at[left, src]
        from_right = full_ref.at[right, src]
        pltpu.make_async_copy(from_left, from_left, left_recv.at[k]).wait()
        pltpu.make_async_copy(from_right, from_right, right_recv.at[k]).wait()
        block, side = ((from_left, right), (from_right, left))[way]
        pltpu.make_async_remote_copy(
            src_ref=block,
            dst_ref=block,
            send_sem=relay_send.at[way],
            recv_sem=relay_recv.at[way],
            device_id={"tp": side},
            device_id_type=MESH,
        ).start()

    def drain(ref, sem):
        pltpu.make_async_copy(ref, ref, sem).wait()

    def pairs(low, high, step):
        def both(i, carry):
            for way in range(2):
                step(2 * i + way, way)
            return carry

        lax.fori_loop(low // 2, high // 2, both, 0)

    def first(k, carry):
        post(k)
        return carry

    def opening(k, way):
        post(k + ahead)
        spread(k)

    def middle(k, way):
        post(k + ahead)
        spread(k)
        relay(k - lag, way)

    def closing(k, way):
        spread(k)
        relay(k - lag, way)

    ahead, lag = min(AHEAD, eps // 2), min(LAG, eps // 2)
    lax.fori_loop(1, ahead, first, 0)
    lax.fori_loop(1, span, meta_near, 0)
    pairs(0, lag, opening)
    pairs(lag, eps - ahead, middle)
    own_meta.wait()
    near = metas_ref.at[pl.ds(0, span - 1)]
    drain(near, meta_recv.at[0])
    lax.fori_loop(1, rows, meta_far, 0)
    pairs(eps - ahead, eps, closing)
    pairs(eps - lag, eps, relay)
    drain(near, meta_send.at[0])
    far = metas_ref.at[pl.ds(0, (rows - 1) * span)]
    drain(far, meta_send.at[1])
    drain(far, meta_recv.at[1])
    drain(send_ref.at[pl.ds(0, eps - 1)], send_sem)
    drain(send_ref, right_send)
    drain(send_ref, left_send)
    half = send_ref.at[pl.ds(0, eps // 2)]
    for way in range(2):
        drain(half, relay_send.at[way])
        drain(half, relay_recv.at[way])


def dispatch(send, meta, eps, tps):
    dma = pltpu.SemaphoreType.DMA
    return pl.pallas_call(
        functools.partial(dispatch_kernel, eps, tps),
        out_shape=(
            jax.ShapeDtypeStruct((tps,) + send.shape, send.dtype),
            jax.ShapeDtypeStruct((eps,) + meta.shape, meta.dtype),
        ),
        in_specs=[pl.BlockSpec(memory_space=pl.ANY)] * 2,
        out_specs=(pl.BlockSpec(memory_space=pl.ANY),) * 2,
        scratch_shapes=[
            dma, dma, dma((2,)), dma((2,)), dma((eps,)), dma, dma, dma((eps,)), dma((eps,)), dma((2,)), dma((2,))
        ],
        compiler_params=pltpu.CompilerParams(collective_id=1, has_side_effects=True),
        name="dispatch",
    )(send, meta)


def experts_kernel(
    eps,
    tps,
    tiles,
    inverse_ref,
    full_ref,
    gain_ref,
    gate_ref,
    up_ref,
    down_ref,
    came_ref,
    act_ref,
    value_ref,
    back_ref,
    send_sem,
    recv_sem,
    relay_send,
    relay_recv,
    own_sem,
    back_send,
    back_recv,
):
    ep = lax.axis_index("ep")
    tp = lax.axis_index("tp")
    right = lax.rem(tp + 1, tps)
    left = lax.rem(tp + tps - 1, tps)
    sides = (right, left)
    parts, sources, cap, width = full_ref.shape
    chunk = sources // tiles
    rows = chunk * cap
    ff = act_ref.shape[1]
    barrier = pltpu.get_barrier_semaphore()

    def greet(k, carry):
        pl.semaphore_signal(
            barrier, inc=1, device_id={"ep": lax.rem(ep + k, eps)}, device_id_type=MESH
        )
        return carry

    for side in sides:
        pl.semaphore_signal(barrier, inc=1, device_id={"tp": side}, device_id_type=MESH)
    lax.fori_loop(1, eps, greet, 0)

    def span(i):
        return pl.ds(i * rows if isinstance(i, int) else pl.multiple_of(i * rows, rows), rows)

    def enter(i, carry):
        wide = [
            full_ref[p, pl.ds(i * chunk, chunk)].astype(jnp.float32).reshape(rows, width)
            for p in range(parts)
        ]
        squares = sum(jnp.sum(part * part, axis=1, keepdims=True) for part in wide)
        factor = lax.rsqrt(squares / (parts * width) + 1e-06)
        normed = jnp.concatenate(
            [
                (part * factor * gain_ref[:, p * width : (p + 1) * width]).astype(jnp.bfloat16)
                for p, part in enumerate(wide)
            ],
            axis=1,
        )
        dims = (((1,), (1,)), ((), ()))
        gate = lax.dot_general(gate_ref[...], normed, dims, preferred_element_type=jnp.float32)
        up = lax.dot_general(up_ref[...], normed, dims, preferred_element_type=jnp.float32)
        act_ref[tp, :, span(i)] = (gate / (1.0 + jnp.exp(-gate)) * up).astype(jnp.bfloat16)
        return carry

    lax.fori_loop(0, tiles, enter, 0)
    pl.semaphore_wait(barrier, eps + 1)
    copies = []
    for c in range(tiles):
        pair = []
        for way in range(2):
            block = act_ref.at[tp, :, span(c)]
            copy = pltpu.make_async_remote_copy(
                src_ref=block,
                dst_ref=block,
                send_sem=send_sem.at[way, c],
                recv_sem=recv_sem.at[way, c],
                device_id={"tp": sides[way]},
                device_id_type=MESH,
            )
            copy.start()
            pair.append(copy)
        copies.append(pair)
    relays = []
    for c in range(tiles):
        way = c % 2
        for pair in copies[c]:
            pair.wait_recv()
        block = act_ref.at[(left, right)[way], :, span(c)]
        copy = pltpu.make_async_remote_copy(
            src_ref=block,
            dst_ref=block,
            send_sem=relay_send.at[c],
            recv_sem=relay_recv.at[c],
            device_id={"tp": sides[way]},
            device_id_type=MESH,
        )
        copy.start()
        relays.append(copy)
    for c in range(tiles):
        relays[c].wait_recv()
        act = jnp.concatenate([act_ref[p, :, span(c)] for p in range(parts)], axis=0)
        value = lax.dot_general(
            act, down_ref[...], (((0,), (0,)), ((), ())), preferred_element_type=jnp.float32
        )
        part = pl.ds(c * chunk, chunk)
        value = value.reshape(chunk, cap, width) + full_ref[tp, part].astype(jnp.float32)
        value_ref[part] = value.astype(jnp.bfloat16)

    def place(d, carry):
        back_ref[d] = value_ref[inverse_ref[d]]
        return carry

    lax.fori_loop(0, eps, place, 0)

    def post(k, carry):
        dst = lax.rem(ep + lax.rem(k * STRIDE, eps), eps)
        pltpu.make_async_remote_copy(
            src_ref=back_ref.at[dst],
            dst_ref=came_ref.at[ep],
            send_sem=back_send,
            recv_sem=back_recv,
            device_id={"ep": dst},
            device_id_type=MESH,
        ).start()
        return carry

    lax.fori_loop(1, eps, post, 0)
    own = pltpu.make_async_copy(back_ref.at[ep], came_ref.at[ep], own_sem)
    own.start()
    for pair in copies:
        for copy in pair:
            copy.wait_send()
    for copy in relays:
        copy.wait_send()
    own.wait()
    most = back_ref.at[pl.ds(0, eps - 1)]
    pltpu.make_async_copy(most, most, back_send).wait()
    pltpu.make_async_copy(most, most, back_recv).wait()


def experts(inverse, full, gain, gate, up, down, eps, tps):
    parts, sources, cap, width = full.shape
    tiles = 4 if sources >= 64 else 2
    dma = pltpu.SemaphoreType.DMA
    vmem = pl.BlockSpec(memory_space=pltpu.VMEM)
    block = (sources, cap, width)
    return pl.pallas_call(
        functools.partial(experts_kernel, eps, tps, tiles),
        out_shape=jax.ShapeDtypeStruct(block, jnp.bfloat16),
        in_specs=[pl.BlockSpec(memory_space=pltpu.SMEM)] + [vmem] * 5,
        out_specs=vmem,
        scratch_shapes=[
            pltpu.VMEM((parts, gate.shape[0], sources * cap), jnp.bfloat16),
            pltpu.VMEM(block, jnp.bfloat16),
            pltpu.VMEM(block, jnp.bfloat16),
            dma((2, tiles)),
            dma((2, tiles)),
            dma((tiles,)),
            dma((tiles,)),
            dma,
            dma,
            dma,
        ],
        compiler_params=pltpu.CompilerParams(collective_id=2, has_side_effects=True),
        name="experts",
    )(inverse, full, gain, gate, up, down)


def combine_kernel(tokens, inverse_ref, ep_ref, meta_ref, came_ref, out_ref):
    count, cap, width = came_ref.shape
    meta = meta_ref[...].astype(jnp.float32)
    top = meta.shape[0] // 2
    _, weighted = slot_matrices(meta[:top, :tokens], meta[top:, :tokens], count)
    rows = came_ref[...].astype(jnp.float32).reshape(count * cap, width).astype(jnp.bfloat16)
    out_ref[...] = lax.dot_general(
        weighted, rows, (((0,), (0,)), ((), ())), preferred_element_type=jnp.float32
    ).astype(jnp.bfloat16)


def combine(inverse, ep, metas, came, tokens):
    return pl.pallas_call(
        functools.partial(combine_kernel, tokens),
        grid_spec=pltpu.PrefetchScalarGridSpec(
            num_scalar_prefetch=2,
            grid=(1,),
            in_specs=[
                pl.BlockSpec((None,) + metas.shape[1:], lambda i, v, e: (v[e[0]], 0, 0)),
                pl.BlockSpec(came.shape, lambda i, v, e: (0, 0, 0)),
            ],
            out_specs=pl.BlockSpec((tokens, came.shape[2]), lambda i, v, e: (0, 0)),
        ),
        out_shape=jax.ShapeDtypeStruct((tokens, came.shape[2]), jnp.bfloat16),
        name="combine",
    )(inverse, ep, metas, came)


def shards(
    queries,
    new_keys,
    new_values,
    key_cache,
    value_cache,
    cache_lengths,
    request_order,
    residual,
    out_weight,
    norm_gain,
    route_experts,
    route_weights,
    expert_gate,
    expert_up,
    expert_down,
):
    tps = lax.axis_size("tp")
    eps = lax.axis_size("ep")
    ep = lax.axis_index("ep")
    context = attention_block(
        queries, new_keys, new_values, key_cache, value_cache, cache_lengths, KVHEADS // tps
    )
    head_terms = jnp.dot(context, out_weight, preferred_element_type=jnp.float32)
    terms = exchange(head_terms.astype(jnp.bfloat16), tps)
    places = jnp.arange(eps, dtype=jnp.int32)
    inverse = jnp.sum(
        jnp.where(request_order[None, :] == places[:, None], places[None, :], 0), axis=1
    )
    send, meta = prepare(terms, residual, route_experts.T, route_weights.T, eps)
    full, metas = dispatch(send, meta, eps, tps)
    came = experts(
        inverse, full, norm_gain[None, :], expert_gate[0].T, expert_up[0].T, expert_down[0], eps, tps
    )
    return combine(inverse, ep[None].astype(jnp.int32), metas, came, route_experts.shape[0])


def solution(mesh):
    return jax.shard_map(
        shards,
        mesh=mesh,
        in_specs=(
            P("ep", "tp"),
            P("ep", "tp"),
            P("ep", "tp"),
            P("ep", None, "tp"),
            P("ep", None, "tp"),
            P("ep"),
            P(),
            P("ep", "tp"),
            P("tp", None),
            P(),
            P("ep", None),
            P("ep", None),
            P("ep", None, "tp"),
            P("ep", None, "tp"),
            P("ep", None, "tp"),
        ),
        out_specs=P("ep", "tp"),
        check_vma=False,
    )
```

```python
import functools
import math

import jax
import jax.numpy as jnp
from jax import lax
from jax.experimental import pallas as pl
from jax.experimental.pallas import tpu as pltpu
from jax.sharding import PartitionSpec as P

HEAD = 128
QHEADS = 16
KVHEADS = 4
CAP = 8
STRIDE = 37
LAG = 32
AHEAD = 48
MESH = pl.DeviceIdType.MESH


def attention_block(queries, new_keys, new_values, key_cache, value_cache, cache_lengths, kv_local):
    tokens_here = queries.shape[0]
    cached = key_cache.shape[1]
    group_size = QHEADS // KVHEADS
    query_view = queries.reshape(tokens_here, kv_local, group_size, HEAD)
    all_keys = jnp.concatenate([key_cache[0], new_keys], axis=0).reshape(
        cached + tokens_here, kv_local, HEAD
    )
    all_values = jnp.concatenate([value_cache[0], new_values], axis=0).reshape(
        cached + tokens_here, kv_local, HEAD
    )
    scores = jnp.einsum(
        "tghd,kgd->tghk", query_view, all_keys, preferred_element_type=jnp.float32
    ) / math.sqrt(HEAD)
    position = jnp.arange(cached + tokens_here, dtype=jnp.int32)
    current = jnp.arange(tokens_here, dtype=jnp.int32)
    visible = jnp.where(
        position[None, :] < cached,
        position[None, :] < cache_lengths[0],
        position[None, :] - cached <= current[:, None],
    )
    visible = visible[:, None, None, :]
    highest = jnp.max(jnp.where(visible, scores, -1e30), axis=-1, keepdims=True)
    raised = jnp.exp(jnp.where(visible, scores - highest, -1e30))
    totals = jnp.sum(raised, axis=-1, keepdims=True)
    weights = raised.astype(jnp.bfloat16)
    context = (
        jnp.einsum("tghk,kgd->tghd", weights, all_values, preferred_element_type=jnp.float32)
        / totals
    )
    return context.astype(jnp.bfloat16).reshape(tokens_here, -1)


def row_span(eps):
    return 16 if eps > 16 else 2


def slot_matrices(experts, mix, count):
    top, tokens = experts.shape
    number = lax.broadcasted_iota(jnp.int32, (count, tokens), 0).astype(jnp.float32)
    named = jnp.zeros((count, tokens), jnp.float32)
    mixed = jnp.zeros((count, tokens), jnp.float32)
    for k in range(top):
        hit = experts[k : k + 1, :] == number
        named = jnp.where(hit, 1.0, named)
        mixed = jnp.where(hit, mix[k : k + 1, :], mixed)
    row = lax.broadcasted_iota(jnp.int32, (tokens, tokens), 0)
    col = lax.broadcasted_iota(jnp.int32, (tokens, tokens), 1)
    earlier = jnp.where(row < col, 1.0, 0.0).astype(jnp.bfloat16)
    rank = jnp.dot(named.astype(jnp.bfloat16), earlier, preferred_element_type=jnp.float32)
    marked = jnp.where(named > 0.0, rank, 255.0).astype(jnp.bfloat16)
    target = lax.broadcasted_iota(jnp.int32, (count * CAP, count), 0)
    source = lax.broadcasted_iota(jnp.int32, (count * CAP, count), 1)
    spread = jnp.where(target // CAP == source, 1.0, 0.0).astype(jnp.bfloat16)
    rank_wide = jnp.dot(spread, marked, preferred_element_type=jnp.float32)
    mix_wide = jnp.dot(spread, mixed.astype(jnp.bfloat16), preferred_element_type=jnp.float32)
    place = lax.rem(
        lax.broadcasted_iota(jnp.int32, (count * CAP, tokens), 0), CAP
    ).astype(jnp.float32)
    chosen = rank_wide == place
    selector = jnp.where(chosen, 1.0, 0.0).astype(jnp.bfloat16)
    weighted = jnp.where(chosen, mix_wide, 0.0).astype(jnp.bfloat16)
    return selector, weighted


def layer_kernel(eps, tps, tiles, *refs):
    (
        inverse_ref,
        terms_ref,
        residual_ref,
        experts_ref,
        weights_ref,
        gain_ref,
        gate_ref,
        up_ref,
        down_ref,
        out_ref,
        got_ref,
        send_ref,
        meta_ref,
        full_ref,
        metas_ref,
        act_ref,
        value_ref,
        back_ref,
        came_ref,
        own_sem,
        term_send,
        term_recv,
        send_sem,
        meta_send,
        meta_recv,
        recv_sem,
        right_send,
        left_send,
        left_recv,
        right_recv,
        relay_send,
        relay_recv,
        act_send,
        act_recv,
        act_relay_send,
        act_relay_recv,
        back_send,
        back_recv,
    ) = refs
    ep = lax.axis_index("ep")
    tp = lax.axis_index("tp")
    right = lax.rem(tp + 1, tps)
    left = lax.rem(tp + tps - 1, tps)
    sides = (right, left)
    tokens, features = residual_ref.shape
    top = experts_ref.shape[0]
    barrier = pltpu.get_barrier_semaphore()

    def greet(k, carry):
        pl.semaphore_signal(
            barrier, inc=1, device_id={"ep": lax.rem(ep + k, eps)}, device_id_type=MESH
        )
        return carry

    for o in range(1, tps):
        pl.semaphore_signal(
            barrier, inc=1, device_id={"tp": lax.rem(tp + o, tps)}, device_id_type=MESH
        )
    lax.fori_loop(1, eps, greet, 0)

    def columns(p):
        return terms_ref.at[:, pl.ds(pl.multiple_of(p * features, features), features)]

    own_terms = pltpu.make_async_copy(columns(tp), got_ref.at[0], own_sem.at[0])
    own_terms.start()
    named = experts_ref[...].astype(jnp.float32)
    weights = weights_ref[...]
    mix = weights / jnp.sum(weights, axis=0, keepdims=True)
    meta_ref[...] = jnp.zeros_like(meta_ref)
    meta_ref[:, :tokens] = jnp.concatenate([named, mix], axis=0).astype(jnp.bfloat16)
    selector, _ = slot_matrices(named, mix, eps)
    pl.semaphore_wait(barrier, eps + tps - 2)
    exchanged = []
    for o in range(1, tps):
        peer = lax.rem(tp + o, tps)
        copy = pltpu.make_async_remote_copy(
            src_ref=columns(peer),
            dst_ref=got_ref.at[o],
            send_sem=term_send.at[o - 1],
            recv_sem=term_recv.at[o - 1],
            device_id={"tp": peer},
            device_id_type=MESH,
        )
        copy.start()
        exchanged.append(copy)
    own_terms.wait()
    for copy in exchanged:
        copy.wait()
    total = residual_ref[...].astype(jnp.float32)
    for o in range(tps):
        total = total + got_ref[o].astype(jnp.float32)
    picked = jnp.dot(selector, total.astype(jnp.bfloat16), preferred_element_type=jnp.float32)
    send_ref[...] = picked.reshape(send_ref.shape).astype(jnp.bfloat16)
    own = pltpu.make_async_copy(send_ref.at[ep], full_ref.at[tp, ep], recv_sem.at[0])
    own.start()
    own_meta = pltpu.make_async_copy(meta_ref, metas_ref.at[ep], own_sem.at[1])
    own_meta.start()
    wide = row_span(eps)
    rows = eps // wide
    row = lax.div(ep, wide)
    place = lax.rem(ep, wide)

    def offset(k):
        return lax.rem(k * STRIDE, eps)

    def source(k):
        return lax.rem(ep + eps - offset(k), eps)

    def post(k):
        off = offset(k)
        dst = lax.rem(ep + off, eps)
        pltpu.make_async_remote_copy(
            src_ref=send_ref.at[dst],
            dst_ref=full_ref.at[tp, ep],
            send_sem=send_sem,
            recv_sem=recv_sem.at[off],
            device_id={"ep": dst},
            device_id_type=MESH,
        ).start()

    def meta_near(k, carry):
        pltpu.make_async_remote_copy(
            src_ref=meta_ref,
            dst_ref=metas_ref.at[ep],
            send_sem=meta_send.at[0],
            recv_sem=meta_recv.at[0],
            device_id={"ep": row * wide + lax.rem(place + k, wide)},
            device_id_type=MESH,
        ).start()
        return carry

    def meta_far(k, carry):
        ours = metas_ref.at[pl.ds(row * wide, wide)]
        pltpu.make_async_remote_copy(
            src_ref=ours,
            dst_ref=ours,
            send_sem=meta_send.at[1],
            recv_sem=meta_recv.at[1],
            device_id={"ep": lax.rem(row + k, rows) * wide + place},
            device_id_type=MESH,
        ).start()
        return carry

    def spread(k):
        block = full_ref.at[tp, source(k)]
        pltpu.make_async_copy(block, block, recv_sem.at[offset(k)]).wait()
        for side, ssem, rsem in ((right, right_send, left_recv), (left, left_send, right_recv)):
            pltpu.make_async_remote_copy(
                src_ref=block,
                dst_ref=block,
                send_sem=ssem,
                recv_sem=rsem.at[k],
                device_id={"tp": side},
                device_id_type=MESH,
            ).start()

    def relay(k, way):
        src = source(k)
        from_left = full_ref.at[left, src]
        from_right = full_ref.at[right, src]
        pltpu.make_async_copy(from_left, from_left, left_recv.at[k]).wait()
        pltpu.make_async_copy(from_right, from_right, right_recv.at[k]).wait()
        block, side = ((from_left, right), (from_right, left))[way]
        pltpu.make_async_remote_copy(
            src_ref=block,
            dst_ref=block,
            send_sem=relay_send.at[way],
            recv_sem=relay_recv.at[way],
            device_id={"tp": side},
            device_id_type=MESH,
        ).start()

    def drain(ref, sem):
        pltpu.make_async_copy(ref, ref, sem).wait()

    def pairs(low, high, step):
        def both(i, carry):
            for way in range(2):
                step(2 * i + way, way)
            return carry

        lax.fori_loop(low // 2, high // 2, both, 0)

    def first(k, carry):
        post(k)
        return carry

    def opening(k, way):
        post(k + ahead)
        spread(k)

    def middle(k, way):
        post(k + ahead)
        spread(k)
        relay(k - lag, way)

    def closing(k, way):
        spread(k)
        relay(k - lag, way)

    ahead, lag = min(AHEAD, eps // 2), min(LAG, eps // 2)
    lax.fori_loop(1, ahead, first, 0)
    lax.fori_loop(1, wide, meta_near, 0)
    pairs(0, lag, opening)
    pairs(lag, eps - ahead, middle)
    own_meta.wait()
    near = metas_ref.at[pl.ds(0, wide - 1)]
    drain(near, meta_recv.at[0])
    lax.fori_loop(1, rows, meta_far, 0)
    pairs(eps - ahead, eps, closing)
    pairs(eps - lag, eps, relay)
    drain(near, meta_send.at[0])
    far = metas_ref.at[pl.ds(0, (rows - 1) * wide)]
    drain(far, meta_send.at[1])
    drain(far, meta_recv.at[1])
    drain(send_ref.at[pl.ds(0, eps - 1)], send_sem)
    drain(send_ref, right_send)
    drain(send_ref, left_send)
    half = send_ref.at[pl.ds(0, eps // 2)]
    for way in range(2):
        drain(half, relay_send.at[way])
        drain(half, relay_recv.at[way])

    parts, sources, cap, width = full_ref.shape
    chunk = sources // tiles
    rows = chunk * cap
    ff = act_ref.shape[1]
    def span(i):
        return pl.ds(i * rows if isinstance(i, int) else pl.multiple_of(i * rows, rows), rows)

    def enter(i, carry):
        wide = [
            full_ref[p, pl.ds(i * chunk, chunk)].astype(jnp.float32).reshape(rows, width)
            for p in range(parts)
        ]
        squares = sum(jnp.sum(part * part, axis=1, keepdims=True) for part in wide)
        factor = lax.rsqrt(squares / (parts * width) + 1e-06)
        normed = jnp.concatenate(
            [
                (part * factor * gain_ref[:, p * width : (p + 1) * width]).astype(jnp.bfloat16)
                for p, part in enumerate(wide)
            ],
            axis=1,
        )
        dims = (((1,), (1,)), ((), ()))
        gate = lax.dot_general(gate_ref[...], normed, dims, preferred_element_type=jnp.float32)
        up = lax.dot_general(up_ref[...], normed, dims, preferred_element_type=jnp.float32)
        act_ref[tp, :, span(i)] = (gate / (1.0 + jnp.exp(-gate)) * up).astype(jnp.bfloat16)
        return carry

    lax.fori_loop(0, tiles, enter, 0)
    copies = []
    for c in range(tiles):
        pair = []
        for way in range(2):
            block = act_ref.at[tp, :, span(c)]
            copy = pltpu.make_async_remote_copy(
                src_ref=block,
                dst_ref=block,
                send_sem=act_send.at[way, c],
                recv_sem=act_recv.at[way, c],
                device_id={"tp": sides[way]},
                device_id_type=MESH,
            )
            copy.start()
            pair.append(copy)
        copies.append(pair)
    relays = []
    for c in range(tiles):
        way = c % 2
        for pair in copies[c]:
            pair.wait_recv()
        block = act_ref.at[(left, right)[way], :, span(c)]
        copy = pltpu.make_async_remote_copy(
            src_ref=block,
            dst_ref=block,
            send_sem=act_relay_send.at[c],
            recv_sem=act_relay_recv.at[c],
            device_id={"tp": sides[way]},
            device_id_type=MESH,
        )
        copy.start()
        relays.append(copy)
    for c in range(tiles):
        relays[c].wait_recv()
        act = jnp.concatenate([act_ref[p, :, span(c)] for p in range(parts)], axis=0)
        value = lax.dot_general(
            act, down_ref[...], (((0,), (0,)), ((), ())), preferred_element_type=jnp.float32
        )
        part = pl.ds(c * chunk, chunk)
        value = value.reshape(chunk, cap, width) + full_ref[tp, part].astype(jnp.float32)
        value_ref[part] = value.astype(jnp.bfloat16)

    def arrange(d, carry):
        back_ref[d] = value_ref[inverse_ref[d]]
        return carry

    lax.fori_loop(0, eps, arrange, 0)

    def post_back(k, carry):
        dst = lax.rem(ep + lax.rem(k * STRIDE, eps), eps)
        pltpu.make_async_remote_copy(
            src_ref=back_ref.at[dst],
            dst_ref=came_ref.at[ep],
            send_sem=back_send,
            recv_sem=back_recv,
            device_id={"ep": dst},
            device_id_type=MESH,
        ).start()
        return carry

    lax.fori_loop(1, eps, post_back, 0)
    own = pltpu.make_async_copy(back_ref.at[ep], came_ref.at[ep], own_sem.at[2])
    own.start()
    theirs = metas_ref[inverse_ref[ep]].astype(jnp.float32)
    _, weighted = slot_matrices(theirs[:top, :tokens], theirs[top:, :tokens], eps)
    for pair in copies:
        for copy in pair:
            copy.wait_send()
    for copy in relays:
        copy.wait_send()
    own.wait()
    most = back_ref.at[pl.ds(0, eps - 1)]
    pltpu.make_async_copy(most, most, back_send).wait()
    pltpu.make_async_copy(most, most, back_recv).wait()
    came = came_ref[...].astype(jnp.float32).reshape(eps * cap, width).astype(jnp.bfloat16)
    out_ref[...] = lax.dot_general(
        weighted, came, (((0,), (0,)), ((), ())), preferred_element_type=jnp.float32
    ).astype(jnp.bfloat16)


def layer(inverse, terms, residual, experts, weights, gain, gate, up, down, eps, tps):
    tokens, width = residual.shape
    tiles = 4 if eps >= 64 else 2
    dma = pltpu.SemaphoreType.DMA
    vmem = pl.BlockSpec(memory_space=pltpu.VMEM)
    meta = (2 * experts.shape[0], 128)

    def room(*shape):
        return pltpu.VMEM(shape, jnp.bfloat16)

    return pl.pallas_call(
        functools.partial(layer_kernel, eps, tps, tiles),
        out_shape=jax.ShapeDtypeStruct((tokens, width), jnp.bfloat16),
        in_specs=[pl.BlockSpec(memory_space=pltpu.SMEM)] + [vmem] * 8,
        out_specs=vmem,
        scratch_shapes=[
            room(tps, tokens, width),
            room(eps, CAP, width),
            room(*meta),
            room(tps, eps, CAP, width),
            room(eps, *meta),
            room(tps, gate.shape[0], eps * CAP),
            room(eps, CAP, width),
            room(eps, CAP, width),
            room(eps, CAP, width),
            dma((3,)),
            dma((tps - 1,)),
            dma((tps - 1,)),
            dma,
            dma((2,)),
            dma((2,)),
            dma((eps,)),
            dma,
            dma,
            dma((eps,)),
            dma((eps,)),
            dma((2,)),
            dma((2,)),
            dma((2, tiles)),
            dma((2, tiles)),
            dma((tiles,)),
            dma((tiles,)),
            dma,
            dma,
        ],
        compiler_params=pltpu.CompilerParams(collective_id=0, has_side_effects=True),
        name="layer",
    )(inverse, terms, residual, experts, weights, gain, gate, up, down)


def shards(
    queries,
    new_keys,
    new_values,
    key_cache,
    value_cache,
    cache_lengths,
    request_order,
    residual,
    out_weight,
    norm_gain,
    route_experts,
    route_weights,
    expert_gate,
    expert_up,
    expert_down,
):
    tps = lax.axis_size("tp")
    eps = lax.axis_size("ep")
    context = attention_block(
        queries, new_keys, new_values, key_cache, value_cache, cache_lengths, KVHEADS // tps
    )
    head_terms = jnp.dot(context, out_weight, preferred_element_type=jnp.float32)
    places = jnp.arange(eps, dtype=jnp.int32)
    inverse = jnp.sum(
        jnp.where(request_order[None, :] == places[:, None], places[None, :], 0), axis=1
    )
    return layer(
        inverse,
        head_terms.astype(jnp.bfloat16),
        residual,
        route_experts.T,
        route_weights.T,
        norm_gain[None, :],
        expert_gate[0].T,
        expert_up[0].T,
        expert_down[0],
        eps,
        tps,
    )


def solution(mesh):
    return jax.shard_map(
        shards,
        mesh=mesh,
        in_specs=(
            P("ep", "tp"),
            P("ep", "tp"),
            P("ep", "tp"),
            P("ep", None, "tp"),
            P("ep", None, "tp"),
            P("ep"),
            P(),
            P("ep", "tp"),
            P("tp", None),
            P(),
            P("ep", None),
            P("ep", None),
            P("ep", None, "tp"),
            P("ep", None, "tp"),
            P("ep", None, "tp"),
        ),
        out_specs=P("ep", "tp"),
        check_vma=False,
    )
```

```python
import functools
import math

import jax
import jax.numpy as jnp
from jax import lax
from jax.experimental import pallas as pl
from jax.experimental.pallas import tpu as pltpu
from jax.sharding import PartitionSpec as P

HEAD = 128
QHEADS = 16
KVHEADS = 4
CAP = 8
STRIDE = 37
LAG = 32
AHEAD = 48
MESH = pl.DeviceIdType.MESH


def attention_block(queries, new_keys, new_values, key_cache, value_cache, cache_lengths, kv_local):
    tokens_here = queries.shape[0]
    cached = key_cache.shape[1]
    group_size = QHEADS // KVHEADS
    query_view = queries.reshape(tokens_here, kv_local, group_size, HEAD)
    all_keys = jnp.concatenate([key_cache[0], new_keys], axis=0).reshape(
        cached + tokens_here, kv_local, HEAD
    )
    all_values = jnp.concatenate([value_cache[0], new_values], axis=0).reshape(
        cached + tokens_here, kv_local, HEAD
    )
    scores = jnp.einsum(
        "tghd,kgd->tghk", query_view, all_keys, preferred_element_type=jnp.float32
    ) / math.sqrt(HEAD)
    position = jnp.arange(cached + tokens_here, dtype=jnp.int32)
    current = jnp.arange(tokens_here, dtype=jnp.int32)
    visible = jnp.where(
        position[None, :] < cached,
        position[None, :] < cache_lengths[0],
        position[None, :] - cached <= current[:, None],
    )
    visible = visible[:, None, None, :]
    highest = jnp.max(jnp.where(visible, scores, -1e30), axis=-1, keepdims=True)
    raised = jnp.exp(jnp.where(visible, scores - highest, -1e30))
    totals = jnp.sum(raised, axis=-1, keepdims=True)
    weights = raised.astype(jnp.bfloat16)
    context = (
        jnp.einsum("tghk,kgd->tghd", weights, all_values, preferred_element_type=jnp.float32)
        / totals
    )
    return context.astype(jnp.bfloat16).reshape(tokens_here, -1)


def row_span(eps):
    return 16 if eps > 16 else 2


def slot_matrices(experts, mix, count):
    top, tokens = experts.shape
    number = lax.broadcasted_iota(jnp.int32, (count, tokens), 0).astype(jnp.float32)
    named = jnp.zeros((count, tokens), jnp.float32)
    mixed = jnp.zeros((count, tokens), jnp.float32)
    for k in range(top):
        hit = experts[k : k + 1, :] == number
        named = jnp.where(hit, 1.0, named)
        mixed = jnp.where(hit, mix[k : k + 1, :], mixed)
    row = lax.broadcasted_iota(jnp.int32, (tokens, tokens), 0)
    col = lax.broadcasted_iota(jnp.int32, (tokens, tokens), 1)
    earlier = jnp.where(row < col, 1.0, 0.0).astype(jnp.bfloat16)
    rank = jnp.dot(named.astype(jnp.bfloat16), earlier, preferred_element_type=jnp.float32)
    marked = jnp.where(named > 0.0, rank, 255.0).astype(jnp.bfloat16)
    target = lax.broadcasted_iota(jnp.int32, (count * CAP, count), 0)
    source = lax.broadcasted_iota(jnp.int32, (count * CAP, count), 1)
    spread = jnp.where(target // CAP == source, 1.0, 0.0).astype(jnp.bfloat16)
    rank_wide = jnp.dot(spread, marked, preferred_element_type=jnp.float32)
    mix_wide = jnp.dot(spread, mixed.astype(jnp.bfloat16), preferred_element_type=jnp.float32)
    place = lax.rem(
        lax.broadcasted_iota(jnp.int32, (count * CAP, tokens), 0), CAP
    ).astype(jnp.float32)
    chosen = rank_wide == place
    selector = jnp.where(chosen, 1.0, 0.0).astype(jnp.bfloat16)
    weighted = jnp.where(chosen, mix_wide, 0.0).astype(jnp.bfloat16)
    return selector, weighted


def layer_kernel(eps, tps, tiles, *refs):
    (
        inverse_ref,
        terms_ref,
        residual_ref,
        experts_ref,
        weights_ref,
        gain_ref,
        gate_ref,
        up_ref,
        down_ref,
        out_ref,
        got_ref,
        send_ref,
        meta_ref,
        full_ref,
        metas_ref,
        act_ref,
        value_ref,
        back_ref,
        came_ref,
        own_sem,
        term_send,
        term_recv,
        send_sem,
        meta_send,
        meta_recv,
        recv_sem,
        right_send,
        left_send,
        left_recv,
        right_recv,
        relay_send,
        relay_recv,
        act_send,
        act_recv,
        act_relay_send,
        act_relay_recv,
        back_send,
        back_recv,
    ) = refs
    ep = lax.axis_index("ep")
    tp = lax.axis_index("tp")
    right = lax.rem(tp + 1, tps)
    left = lax.rem(tp + tps - 1, tps)
    sides = (right, left)
    tokens, features = residual_ref.shape
    top = experts_ref.shape[0]
    barrier = pltpu.get_barrier_semaphore()

    def greet(k, carry):
        pl.semaphore_signal(
            barrier, inc=1, device_id={"ep": lax.rem(ep + k, eps)}, device_id_type=MESH
        )
        return carry

    for o in range(1, tps):
        pl.semaphore_signal(
            barrier, inc=1, device_id={"tp": lax.rem(tp + o, tps)}, device_id_type=MESH
        )
    lax.fori_loop(1, eps, greet, 0)

    def columns(p):
        return terms_ref.at[:, pl.ds(pl.multiple_of(p * features, features), features)]

    own_terms = pltpu.make_async_copy(columns(tp), got_ref.at[0], own_sem.at[0])
    own_terms.start()
    named = experts_ref[...].astype(jnp.float32)
    weights = weights_ref[...]
    mix = weights / jnp.sum(weights, axis=0, keepdims=True)
    meta_ref[...] = jnp.zeros_like(meta_ref)
    meta_ref[:, :tokens] = jnp.concatenate([named, mix], axis=0).astype(jnp.bfloat16)
    selector, _ = slot_matrices(named, mix, eps)
    pl.semaphore_wait(barrier, eps + tps - 2)
    exchanged = []
    for o in range(1, tps):
        peer = lax.rem(tp + o, tps)
        copy = pltpu.make_async_remote_copy(
            src_ref=columns(peer),
            dst_ref=got_ref.at[o],
            send_sem=term_send.at[o - 1],
            recv_sem=term_recv.at[o - 1],
            device_id={"tp": peer},
            device_id_type=MESH,
        )
        copy.start()
        exchanged.append(copy)
    own_terms.wait()
    for copy in exchanged:
        copy.wait()
    total = residual_ref[...].astype(jnp.float32)
    for o in range(tps):
        total = total + got_ref[o].astype(jnp.float32)
    picked = jnp.dot(selector, total.astype(jnp.bfloat16), preferred_element_type=jnp.float32)
    send_ref[...] = picked.reshape(send_ref.shape).astype(jnp.bfloat16)
    own = pltpu.make_async_copy(send_ref.at[ep], full_ref.at[tp, ep], recv_sem.at[0])
    own.start()
    own_meta = pltpu.make_async_copy(meta_ref, metas_ref.at[ep], own_sem.at[1])
    own_meta.start()
    wide = row_span(eps)
    rows = eps // wide
    row = lax.div(ep, wide)
    place = lax.rem(ep, wide)

    def offset(k):
        return lax.rem(k * STRIDE, eps)

    def source(k):
        return lax.rem(ep + eps - offset(k), eps)

    def post(k):
        off = offset(k)
        dst = lax.rem(ep + off, eps)
        pltpu.make_async_remote_copy(
            src_ref=send_ref.at[dst],
            dst_ref=full_ref.at[tp, ep],
            send_sem=send_sem,
            recv_sem=recv_sem.at[off],
            device_id={"ep": dst},
            device_id_type=MESH,
        ).start()

    def meta_near(k, carry):
        pltpu.make_async_remote_copy(
            src_ref=meta_ref,
            dst_ref=metas_ref.at[ep],
            send_sem=meta_send.at[0],
            recv_sem=meta_recv.at[0],
            device_id={"ep": row * wide + lax.rem(place + k, wide)},
            device_id_type=MESH,
        ).start()
        return carry

    def meta_far(k, carry):
        ours = metas_ref.at[pl.ds(row * wide, wide)]
        pltpu.make_async_remote_copy(
            src_ref=ours,
            dst_ref=ours,
            send_sem=meta_send.at[1],
            recv_sem=meta_recv.at[1],
            device_id={"ep": lax.rem(row + k, rows) * wide + place},
            device_id_type=MESH,
        ).start()
        return carry

    def spread(k):
        block = full_ref.at[tp, source(k)]
        pltpu.make_async_copy(block, block, recv_sem.at[offset(k)]).wait()
        for side, ssem, rsem in ((right, right_send, left_recv), (left, left_send, right_recv)):
            pltpu.make_async_remote_copy(
                src_ref=block,
                dst_ref=block,
                send_sem=ssem,
                recv_sem=rsem.at[k],
                device_id={"tp": side},
                device_id_type=MESH,
            ).start()

    def relay(k, way):
        src = source(k)
        from_left = full_ref.at[left, src]
        from_right = full_ref.at[right, src]
        pltpu.make_async_copy(from_left, from_left, left_recv.at[k]).wait()
        pltpu.make_async_copy(from_right, from_right, right_recv.at[k]).wait()
        block, side = ((from_left, right), (from_right, left))[way]
        pltpu.make_async_remote_copy(
            src_ref=block,
            dst_ref=block,
            send_sem=relay_send.at[way],
            recv_sem=relay_recv.at[way],
            device_id={"tp": side},
            device_id_type=MESH,
        ).start()

    def drain(ref, sem):
        pltpu.make_async_copy(ref, ref, sem).wait()

    def pairs(low, high, step):
        def both(i, carry):
            for way in range(2):
                step(2 * i + way, way)
            return carry

        lax.fori_loop(low // 2, high // 2, both, 0)

    def first(k, carry):
        post(k)
        return carry

    def opening(k, way):
        post(k + ahead)
        spread(k)

    def middle(k, way):
        post(k + ahead)
        spread(k)
        relay(k - lag, way)

    def closing(k, way):
        spread(k)
        relay(k - lag, way)

    ahead, lag = min(AHEAD, eps // 2), min(LAG, eps // 2)
    lax.fori_loop(1, ahead, first, 0)
    lax.fori_loop(1, wide, meta_near, 0)
    pairs(0, lag, opening)
    pairs(lag, eps - ahead, middle)
    own_meta.wait()
    near = metas_ref.at[pl.ds(0, wide - 1)]
    drain(near, meta_recv.at[0])
    lax.fori_loop(1, rows, meta_far, 0)
    pairs(eps - ahead, eps, closing)
    pairs(eps - lag, eps, relay)
    drain(near, meta_send.at[0])
    far = metas_ref.at[pl.ds(0, (rows - 1) * wide)]
    drain(far, meta_send.at[1])
    drain(far, meta_recv.at[1])
    drain(send_ref.at[pl.ds(0, eps - 1)], send_sem)
    drain(send_ref, right_send)
    drain(send_ref, left_send)
    half = send_ref.at[pl.ds(0, eps // 2)]
    for way in range(2):
        drain(half, relay_send.at[way])
        drain(half, relay_recv.at[way])

    parts, sources, cap, width = full_ref.shape
    chunk = sources // tiles
    rows = chunk * cap
    ff = act_ref.shape[1]
    def span(i):
        return pl.ds(i * rows if isinstance(i, int) else pl.multiple_of(i * rows, rows), rows)

    def enter(i, carry):
        wide = [
            full_ref[p, pl.ds(i * chunk, chunk)].astype(jnp.float32).reshape(rows, width)
            for p in range(parts)
        ]
        squares = sum(jnp.sum(part * part, axis=1, keepdims=True) for part in wide)
        factor = lax.rsqrt(squares / (parts * width) + 1e-06)
        normed = jnp.concatenate(
            [
                (part * factor * gain_ref[:, p * width : (p + 1) * width]).astype(jnp.bfloat16)
                for p, part in enumerate(wide)
            ],
            axis=1,
        )
        dims = (((1,), (1,)), ((), ()))
        gate = lax.dot_general(gate_ref[...], normed, dims, preferred_element_type=jnp.float32)
        up = lax.dot_general(up_ref[...], normed, dims, preferred_element_type=jnp.float32)
        act_ref[tp, :, span(i)] = (gate / (1.0 + jnp.exp(-gate)) * up).astype(jnp.bfloat16)
        return carry

    copies = []
    for c in range(tiles):
        enter(c, 0)
        pair = []
        for way in range(2):
            block = act_ref.at[tp, :, span(c)]
            copy = pltpu.make_async_remote_copy(
                src_ref=block,
                dst_ref=block,
                send_sem=act_send.at[way, c],
                recv_sem=act_recv.at[way, c],
                device_id={"tp": sides[way]},
                device_id_type=MESH,
            )
            copy.start()
            pair.append(copy)
        copies.append(pair)
    relays = []
    for c in range(tiles):
        way = c % 2
        for pair in copies[c]:
            pair.wait_recv()
        block = act_ref.at[(left, right)[way], :, span(c)]
        copy = pltpu.make_async_remote_copy(
            src_ref=block,
            dst_ref=block,
            send_sem=act_relay_send.at[c],
            recv_sem=act_relay_recv.at[c],
            device_id={"tp": sides[way]},
            device_id_type=MESH,
        )
        copy.start()
        relays.append(copy)
    for c in range(tiles):
        relays[c].wait_recv()
        act = jnp.concatenate([act_ref[p, :, span(c)] for p in range(parts)], axis=0)
        value = lax.dot_general(
            act, down_ref[...], (((0,), (0,)), ((), ())), preferred_element_type=jnp.float32
        )
        part = pl.ds(c * chunk, chunk)
        value = value.reshape(chunk, cap, width) + full_ref[tp, part].astype(jnp.float32)
        value_ref[part] = value.astype(jnp.bfloat16)

    def arrange(d, carry):
        back_ref[d] = value_ref[inverse_ref[d]]
        return carry

    lax.fori_loop(0, eps, arrange, 0)

    def post_back(k, carry):
        dst = lax.rem(ep + lax.rem(k * STRIDE, eps), eps)
        pltpu.make_async_remote_copy(
            src_ref=back_ref.at[dst],
            dst_ref=came_ref.at[ep],
            send_sem=back_send,
            recv_sem=back_recv,
            device_id={"ep": dst},
            device_id_type=MESH,
        ).start()
        return carry

    lax.fori_loop(1, eps, post_back, 0)
    own = pltpu.make_async_copy(back_ref.at[ep], came_ref.at[ep], own_sem.at[2])
    own.start()
    theirs = metas_ref[inverse_ref[ep]].astype(jnp.float32)
    _, weighted = slot_matrices(theirs[:top, :tokens], theirs[top:, :tokens], eps)
    for pair in copies:
        for copy in pair:
            copy.wait_send()
    for copy in relays:
        copy.wait_send()
    own.wait()
    most = back_ref.at[pl.ds(0, eps - 1)]
    pltpu.make_async_copy(most, most, back_send).wait()
    pltpu.make_async_copy(most, most, back_recv).wait()
    came = came_ref[...].astype(jnp.float32).reshape(eps * cap, width).astype(jnp.bfloat16)
    out_ref[...] = lax.dot_general(
        weighted, came, (((0,), (0,)), ((), ())), preferred_element_type=jnp.float32
    ).astype(jnp.bfloat16)


def layer(inverse, terms, residual, experts, weights, gain, gate, up, down, eps, tps):
    tokens, width = residual.shape
    tiles = 4 if eps >= 64 else 2
    dma = pltpu.SemaphoreType.DMA
    vmem = pl.BlockSpec(memory_space=pltpu.VMEM)
    meta = (2 * experts.shape[0], 128)

    def room(*shape):
        return pltpu.VMEM(shape, jnp.bfloat16)

    return pl.pallas_call(
        functools.partial(layer_kernel, eps, tps, tiles),
        out_shape=jax.ShapeDtypeStruct((tokens, width), jnp.bfloat16),
        in_specs=[pl.BlockSpec(memory_space=pltpu.SMEM)] + [vmem] * 8,
        out_specs=vmem,
        scratch_shapes=[
            room(tps, tokens, width),
            room(eps, CAP, width),
            room(*meta),
            room(tps, eps, CAP, width),
            room(eps, *meta),
            room(tps, gate.shape[0], eps * CAP),
            room(eps, CAP, width),
            room(eps, CAP, width),
            room(eps, CAP, width),
            dma((3,)),
            dma((tps - 1,)),
            dma((tps - 1,)),
            dma,
            dma((2,)),
            dma((2,)),
            dma((eps,)),
            dma,
            dma,
            dma((eps,)),
            dma((eps,)),
            dma((2,)),
            dma((2,)),
            dma((2, tiles)),
            dma((2, tiles)),
            dma((tiles,)),
            dma((tiles,)),
            dma,
            dma,
        ],
        compiler_params=pltpu.CompilerParams(collective_id=0, has_side_effects=True),
        name="layer",
    )(inverse, terms, residual, experts, weights, gain, gate, up, down)


def shards(
    queries,
    new_keys,
    new_values,
    key_cache,
    value_cache,
    cache_lengths,
    request_order,
    residual,
    out_weight,
    norm_gain,
    route_experts,
    route_weights,
    expert_gate,
    expert_up,
    expert_down,
):
    tps = lax.axis_size("tp")
    eps = lax.axis_size("ep")
    context = attention_block(
        queries, new_keys, new_values, key_cache, value_cache, cache_lengths, KVHEADS // tps
    )
    head_terms = jnp.dot(context, out_weight, preferred_element_type=jnp.float32)
    places = jnp.arange(eps, dtype=jnp.int32)
    inverse = jnp.sum(
        jnp.where(request_order[None, :] == places[:, None], places[None, :], 0), axis=1
    )
    return layer(
        inverse,
        head_terms.astype(jnp.bfloat16),
        residual,
        route_experts.T,
        route_weights.T,
        norm_gain[None, :],
        expert_gate[0].T,
        expert_up[0].T,
        expert_down[0],
        eps,
        tps,
    )


def solution(mesh):
    return jax.shard_map(
        shards,
        mesh=mesh,
        in_specs=(
            P("ep", "tp"),
            P("ep", "tp"),
            P("ep", "tp"),
            P("ep", None, "tp"),
            P("ep", None, "tp"),
            P("ep"),
            P(),
            P("ep", "tp"),
            P("tp", None),
            P(),
            P("ep", None),
            P("ep", None),
            P("ep", None, "tp"),
            P("ep", None, "tp"),
            P("ep", None, "tp"),
        ),
        out_specs=P("ep", "tp"),
        check_vma=False,
    )
```
